32 devices in a mesh: rows: 16 (over z, y, core), cols: 2 (over x).
Axes of the slice: x: 2, y: 2, z: 4, core: 2. Of those that a mesh axis runs over, the one named last changes fastest.
Arguments:
- sketch: bfloat16 [128, 32768], P('cols', 'rows'), may hold values from -6 to 6
- geometry: float32 [3, 32768], P(None, 'rows'), may hold values from 0 to 32, as said below
- neighbours: int32 [32, 5], replicated, may hold values from 0 to 31, as said below
- counts: int32 [32], replicated, may hold values from 1 to 5, as said below
Outputs:
- modes: float32 [128, 32768], P('cols', 'rows')
The draws below stay inside these ranges and needn't reach their ends.
Inputs may be any that keep to these rules, and one draw needn't show every extreme that they name: `geometry`: row 0 of block b lies in [b, b + 1); row 1 lies in [0, 16); row 2 is positive. `neighbours`: in row r the first counts[r] entries are distinct blocks c with |c - r| <= 2, r itself among them; the remaining entries equal r. `counts`: some row block has all 5 column blocks.
All inputs are finite; a program needn't handle non-finite values.
Results may differ from the reference program's by a relative error of at most 0.0059.
Values may be sent and summed in bfloat16 or wider, within the bound.
A program may use at most 64 MiB of HBM per device.

```python
import math
import jax
import jax.numpy as jnp
from jax import lax

B = 1024
PANEL = 64
NB = 32
N = 32768
SKETCH = 128
REACH = 2
KMAX = 5


def draw_geometry(key, part):
    key_along, key_across, key_area = jax.random.split(key, 3)
    block_pos = (jnp.arange(N) // B).astype(jnp.float32)
    along = block_pos + jax.random.uniform(key_along, (N,), jnp.float32, 0.0, 0.999)
    across = jax.random.uniform(key_across, (N,), jnp.float32, 0.0, 15.99)
    rough = jnp.exp(jax.random.uniform(key_area, (N,), jnp.float32, math.log(0.8), math.log(1.25)))
    taper = 1.0 + 0.5 * block_pos / (NB - 1)
    return jnp.stack([along, across, rough * taper]).astype(jnp.float32)


def pattern_tables(key):
    key = jax.random.fold_in(key, 7)
    key_dense, key_roll, key_full = jax.random.split(key, 3)
    block_ids = jnp.arange(NB, dtype=jnp.int32)[:, None]
    offsets = jnp.arange(KMAX, dtype=jnp.int32)[None, :] - REACH
    column_ids = block_ids + offsets
    dense = jax.random.randint(key_dense, (NB, 1), 0, 4) == 0
    chance = jnp.where(dense, 90, 12)
    rolled = jax.random.randint(key_roll, (NB, KMAX), 0, 100)
    full_row = jax.random.randint(key_full, (), REACH, NB - REACH)
    inside = (column_ids >= 0) & (column_ids < NB)
    chosen = ((rolled < chance) | (offsets == 0) | (block_ids == full_row)) & inside
    ranking = jnp.where(chosen, 0, 2 * KMAX) + jnp.arange(KMAX, dtype=jnp.int32)[None, :]
    order = jnp.argsort(ranking, axis=1)
    listed = jnp.take_along_axis(jnp.where(chosen, column_ids, block_ids), order, axis=1)
    totals = jnp.sum(chosen.astype(jnp.int32), axis=1)
    return (listed.astype(jnp.int32), totals.astype(jnp.int32))


def draw_neighbours(key, part):
    return pattern_tables(key)[0]


def draw_counts(key, part):
    return pattern_tables(key)[1]


def block_levels(key, shape, cuts, smallest, top_value):
    def one(position, shards_of):
        draws = jax.random.uniform(jax.random.fold_in(jax.random.fold_in(key, 6), position), (shards_of,), jnp.float32, smallest / len(cuts), top_value / len(cuts))
        return jnp.repeat(jnp.exp(draws), shape[position] // shards_of).reshape((-1,) + (1,) * (len(shape) - position - 1))

    factor_of = one(*cuts[0])
    for cut in cuts[1:]:
        factor_of = factor_of * one(*cut)
    return factor_of


def bell_draw(own_key, shape, spread, limit, pieces=(), held_as=jnp.bfloat16):
    result = spread * jax.random.normal(own_key, shape, jnp.float32)
    if pieces:
        result = result * block_levels(own_key, shape, pieces, -0.22, 0.18)
    return jnp.clip(result, -limit, limit).astype(held_as)


def setup_inputs(seed: int = 0) -> dict:
    keys = jax.random.split(jax.random.key(seed), 5)
    sketch = bell_draw(keys[0], (SKETCH, N), 1.0, 6.0, ((0, 2), (1, 16)))
    geometry = draw_geometry(jax.random.fold_in(keys[4], 71), 0)
    neighbours = draw_neighbours(jax.random.fold_in(keys[4], 71), 0)
    counts = draw_counts(jax.random.fold_in(keys[4], 71), 0)
    return {"sketch": sketch, "geometry": geometry, "neighbours": neighbours, "counts": counts}


highest = lax.Precision.HIGHEST

def kernel_tile(col_geo, row_geo, wavenumber):
    delta_x = col_geo[0][:, None] - row_geo[0][None, :]
    delta_y = col_geo[1][:, None] - row_geo[1][None, :]
    distance = jnp.sqrt(delta_x * delta_x + delta_y * delta_y)
    weights = col_geo[2][:, None] * row_geo[2][None, :]
    return (weights * jnp.sinc(distance * (wavenumber / math.pi))).astype(jnp.bfloat16)

def apply_operator(panel_t, geometry, neighbours, counts):
    wavenumber = 4.0 * math.sqrt(B)
    blocks = geometry.reshape(3, NB, B)
    columns = panel_t.shape[0]

    def one_block(block_index):
        row_geo = lax.dynamic_index_in_dim(blocks, block_index, 1, keepdims=False)
        running = jnp.zeros((columns, B), jnp.float32)
        for slot_index in range(KMAX):
            column_id = neighbours[block_index, slot_index].astype(jnp.int32)
            col_geo = lax.dynamic_index_in_dim(blocks, column_id, 1, keepdims=False)
            col_panel = lax.dynamic_slice_in_dim(panel_t, (column_id * B).astype(jnp.int32), B, 1)
            tile_term = jnp.dot(col_panel.astype(jnp.float32), kernel_tile(col_geo, row_geo, wavenumber).astype(jnp.float32), preferred_element_type=jnp.float32)
            running = running + jnp.where(slot_index < counts[block_index], tile_term, 0.0)
        return running
    stacked = lax.map(one_block, jnp.arange(NB, dtype=jnp.int32))
    return jnp.transpose(stacked, (1, 0, 2)).reshape(columns, NB * B)

def reference(sketch, geometry, neighbours, counts):
    first_product = apply_operator(sketch, geometry, neighbours, counts).astype(jnp.bfloat16)
    second_product = apply_operator(first_product, geometry, neighbours, counts)
    panels = SKETCH // PANEL
    removed = jnp.zeros_like(second_product)
    mode_rows = []
    for panel_index in range(panels):
        lower_row = panel_index * PANEL
        upper_row = lower_row + PANEL
        current = second_product[lower_row:upper_row] - removed[lower_row:upper_row]
        gram_matrix = jnp.dot(current, current.T, precision=highest)
        cholesky_factor = jnp.linalg.cholesky(gram_matrix)
        basis_rows = lax.linalg.triangular_solve(cholesky_factor, current, left_side=True, lower=True)
        mode_rows.append(basis_rows)
        if panel_index + 1 < panels:
            coefficients = jnp.dot(basis_rows, second_product[upper_row:].T, precision=highest)
            removed = removed.at[upper_row:].add(jnp.dot(coefficients.T, basis_rows, precision=highest))
    return jnp.concatenate(mode_rows, axis=0) * math.sqrt(N)
```

```python
import functools
import math

import jax
import jax.numpy as jnp
from jax import lax
from jax.experimental import pallas as pl
from jax.experimental.pallas import tpu as pltpu
from jax.sharding import PartitionSpec as P

B = 1024
BLK_DEV = 2


highest = lax.Precision.HIGHEST


def padded(shard, sides, width):
    for axis, dim in sides:
        size, length = (lax.axis_size(axis), shard.shape[dim])
        up = [(i, (i + 1) % size) for i in range(size - 1)]
        down = [(j, i) for i, j in up]
        last = lax.slice_in_dim(shard, length - width, length, axis=dim)
        initial = lax.slice_in_dim(shard, 0, width, axis=dim)
        before = lax.ppermute(last, axis, up)
        after = lax.ppermute(initial, axis, down)
        shard = jnp.concatenate([before, shard, after], axis=dim)
    return shard


def spread(value, axis, source):
    kept = jnp.where(lax.axis_index(axis) == source, value, 0).astype(value.dtype)
    return lax.psum(kept, axis)


def kernel_tile(col_geo, row_geo, wavenumber):
    delta_x = col_geo[0][:, None] - row_geo[0][None, :]
    delta_y = col_geo[1][:, None] - row_geo[1][None, :]
    distance = jnp.sqrt(delta_x * delta_x + delta_y * delta_y)
    weights = col_geo[2][:, None] * row_geo[2][None, :]
    return (weights * jnp.sinc(distance * (wavenumber / math.pi))).astype(jnp.bfloat16)


def choose_slice(own_array, start, width):
    own_part = lax.dynamic_slice_in_dim(own_array, start, width, 1)
    return own_part


def task_lists(neighbours, counts, device_index, unit_blocks):
    slot_count = neighbours.shape[1]
    unit_count = unit_blocks.shape[0]
    slot_ids = jnp.arange(slot_count, dtype=jnp.int32)
    owners = jnp.zeros((unit_count,), jnp.int32) + device_index
    row_blocks = owners * BLK_DEV + unit_blocks
    flags = (slot_ids[None, :] < counts[row_blocks][:, None]).astype(jnp.int32).reshape(-1)
    column_ids = neighbours[row_blocks].reshape(-1)
    base_blocks = jnp.repeat(owners * BLK_DEV - BLK_DEV, slot_count)
    starts = (column_ids - base_blocks) * B
    task_total = flags.shape[0]
    task_ids = jnp.arange(task_total, dtype=jnp.int32)
    rank = jnp.cumsum(flags) - flags
    taken = flags == 1
    task_sides = jnp.zeros((task_total,), jnp.int32)
    target = jnp.where(taken, rank, task_total)
    blank = jnp.zeros((task_total + 1,), jnp.int32)
    order_side = blank.at[target].set(task_sides)
    order_unit = blank.at[target].set(task_ids // slot_count % unit_count)
    order_start = blank.at[target].set(starts)
    return (order_side, order_unit, order_start, jnp.sum(taken.astype(jnp.int32)))


def evaluate_tiles(tables, geo_wide, unit_blocks, unit_offset, unit_rows, capacity, wavenumber):
    order_side, order_unit, order_start, own_count = tables

    def add_tile(task, stored):
        row_start = (BLK_DEV + unit_blocks[order_unit[task]]) * B + unit_offset
        row_geo = choose_slice(geo_wide, row_start, unit_rows)
        col_geo = choose_slice(geo_wide, order_start[task], B)
        tile = kernel_tile(col_geo, row_geo, wavenumber)
        return lax.dynamic_update_slice(stored, tile[None], (task, 0, 0))

    initial = jnp.zeros((capacity, B, unit_rows), jnp.bfloat16)
    return lax.fori_loop(0, own_count, add_tile, initial)


def apply_tiles(stored, tables, panel_wide, unit_rows, unit_count):
    order_side, order_unit, order_start, own_count = tables
    columns = panel_wide.shape[0]
    side_count = 1

    def add_term(task, running):
        col_panel = choose_slice(panel_wide, order_start[task], B)
        term = jnp.dot(col_panel, stored[task], preferred_element_type=jnp.float32)
        return running + term[None]

    initial = jnp.zeros((side_count, columns, unit_count * unit_rows), jnp.float32)
    return lax.fori_loop(0, own_count, add_term, initial)


def operator_product(panel_t, stored, tables, unit_rows, unit_count):
    panel_wide = padded(panel_t, (("rows", 1),), BLK_DEV * B)
    gathered = apply_tiles(
        stored,
        tables,
        lax.all_gather(panel_wide, "cols", axis=0, tiled=True),
        unit_rows,
        unit_count,
    )[0]
    return lax.all_to_all(gathered, "cols", split_axis=0, concat_axis=1, tiled=True)


def normalize(current):
    gram_matrix = lax.psum(jnp.dot(current, current.T, precision=highest), "rows")
    cholesky_factor = jnp.linalg.cholesky(gram_matrix)
    return lax.linalg.triangular_solve(cholesky_factor, current, left_side=True, lower=True)


def orthonormal(second_product):
    position = lax.axis_index("cols")
    panels = lax.axis_size("cols")
    norm_scale = math.sqrt(second_product.shape[1] * lax.axis_size("rows"))
    mode_rows = jnp.zeros_like(second_product)
    removed = jnp.zeros_like(second_product)
    for panel_index in range(panels):
        basis_rows = normalize(second_product - removed)
        mode_rows = jnp.where(position == panel_index, basis_rows, mode_rows)
        if panel_index + 1 < panels:
            finished = spread(basis_rows, "cols", panel_index)
            coefficients = lax.psum(jnp.dot(finished, second_product.T, precision=highest), "rows")
            update = jnp.dot(coefficients.T, finished, precision=highest)
            removed = removed + jnp.where(position > panel_index, update, 0.0)
    return mode_rows * norm_scale


def body(sketch, geometry, neighbours, counts):
    wavenumber = 4.0 * math.sqrt(B)
    device_index = lax.axis_index("rows")
    geo_wide = padded(geometry, (("rows", 1),), BLK_DEV * B)
    unit_blocks = jnp.arange(BLK_DEV, dtype=jnp.int32)
    unit_offset = 0
    unit_rows = BLK_DEV * B // lax.axis_size("cols")
    slice_start = lax.axis_index("cols") * unit_rows
    unit_blocks = jnp.reshape(slice_start // B, (1,))
    unit_offset = slice_start % B
    unit_count = unit_blocks.shape[0]
    tables = task_lists(neighbours, counts, device_index, unit_blocks)
    capacity = unit_count * neighbours.shape[1]
    stored = evaluate_tiles(
        tables, geo_wide, unit_blocks, unit_offset, unit_rows, capacity, wavenumber
    )
    first_product = operator_product(sketch, stored, tables, unit_rows, unit_count).astype(
        jnp.bfloat16
    )
    second_product = operator_product(first_product, stored, tables, unit_rows, unit_count)
    return orthonormal(second_product)


MESH = pl.DeviceIdType.MESH
SLOTS = 5
CHUNK = 256
GROUP = 256
SIN = (
    6.28318330620465,
    -41.34144799998349,
    81.59666336606338,
    -76.58390226519525,
    41.21913554078422,
    -12.289783804974757,
)
MAGIC = 12582912.0


def column_range(dq, to_col):
    first = -2 * dq - to_col + 2
    kept = [e for e in range(2) if 0 <= first + e < SLOTS]
    lo, count = kept[0], len(kept)
    return (first + lo) * B, lo * B, count * B


def fast_kernel(
    rows_n,
    wavenumber,
    sketch,
    geometry,
    neighbours_hbm,
    counts_hbm,
    gram,
    second,
    tiles,
    wide,
    geo,
    weight,
    first,
    own_x,
    own_y,
    own_a,
    gram_send,
    gram_recv,
    geo_sem,
    sk_sem,
    first_sem,
    gram_sem,
    pair_sem,
    local_sem,
    neighbours,
    counts,
):
    q = lax.axis_index("rows")
    x = lax.axis_index("cols")
    r = 2 * q + x
    blocks_n = 2 * rows_n
    flips = [1 << k for k in range(rows_n.bit_length() - 1)]

    def partner_q(flip):
        return q + flip - 2 * flip * ((q // flip) % 2)

    barrier = pltpu.get_barrier_semaphore()
    pl.semaphore_signal(barrier, inc=1, device_id=(q, 1 - x), device_id_type=MESH)
    for flip in flips[1:]:
        pl.semaphore_signal(barrier, inc=1, device_id=(partner_q(flip), x), device_id_type=MESH)
    for dq in (-1, 1):

        @pl.when((q + dq >= 0) & (q + dq < rows_n))
        def _(dq=dq):
            pl.semaphore_signal(barrier, inc=1, device_id=(q + dq, x), device_id_type=MESH)

    def local_copy(c, k):
        at = column_range(0, c)[0]
        if k == 0:
            return pltpu.make_async_copy(geometry, geo.at[:, at : at + 2 * B], local_sem.at[0])
        held = wide.at[64 * c : 64 * c + 64, at : at + 2 * B]
        return pltpu.make_async_copy(sketch, held, local_sem.at[1])

    table_copies = (
        pltpu.make_async_copy(neighbours_hbm, neighbours, local_sem.at[2]),
        pltpu.make_async_copy(counts_hbm, counts, local_sem.at[3]),
    )
    for copy in table_copies:
        copy.start()
    for c in range(2):

        @pl.when(x == c)
        def _(c=c):
            local_copy(c, 0).start()
            local_copy(c, 1).start()

    for step in (-2, -1, 1, 2):

        @pl.when((r + step < 0) | (r + step >= blocks_n))
        def _(step=step):
            at = (2 + step) * B
            geo[:, at : at + B] = jnp.full((3, B), -1.0, jnp.float32)
            wide[:, at : at + B] = jnp.zeros((128, B), jnp.bfloat16)
            first[at : at + B, :] = jnp.zeros((B, 128), jnp.bfloat16)

    sides = jnp.where(q > 0, 1, 0) + jnp.where(q < rows_n - 1, 1, 0)
    pl.semaphore_wait(barrier, len(flips) + sides)

    def geo_copy(dq, col):
        to, lo, n = column_range(dq, col)
        k = (dq + 1) // 2
        return pltpu.make_async_remote_copy(
            src_ref=geometry.at[:, lo : lo + n],
            dst_ref=geo.at[:, to : to + n],
            send_sem=geo_sem.at[0, k],
            recv_sem=geo_sem.at[1, k],
            device_id=(q + dq, x),
            device_id_type=MESH,
        )

    def cross_copy(c):
        at = column_range(0, 1 - c)[0]
        return pltpu.make_async_remote_copy(
            src_ref=sketch,
            dst_ref=wide.at[64 * c : 64 * c + 64, at : at + 2 * B],
            send_sem=sk_sem.at[0, 0],
            recv_sem=sk_sem.at[1, 0],
            device_id=(q, 1 - c),
            device_id_type=MESH,
        )

    def side_copy(dq, c, passed_on):
        to, lo, n = column_range(dq, c)
        k = (1 if dq < 0 else 2) + (2 if passed_on else 0)
        panel = 1 - c if passed_on else c
        lines = slice(64 * panel, 64 * panel + 64)
        at = column_range(0, c)[0] + lo
        return pltpu.make_async_remote_copy(
            src_ref=wide.at[lines, at : at + n] if passed_on else sketch.at[:, lo : lo + n],
            dst_ref=wide.at[lines, to : to + n],
            send_sem=sk_sem.at[0, k],
            recv_sem=sk_sem.at[1, k],
            device_id=(q + dq, c),
            device_id_type=MESH,
        )

    def inside(dq):
        return (q + dq >= 0) & (q + dq < rows_n)

    for c in range(2):
        for dq in (-1, 1):

            @pl.when((x == c) & inside(dq))
            def _(c=c, dq=dq):
                geo_copy(dq, c).start()

    for c in range(2):

        @pl.when(x == c)
        def _(c=c):
            cross_copy(c).start()

        for dq in (-1, 1):

            @pl.when((x == c) & inside(dq))
            def _(c=c, dq=dq):
                side_copy(dq, c, False).start()

    def pass_sketch_on():
        for c in range(2):

            @pl.when(x == c)
            def _(c=c):
                cross_copy(1 - c).wait_recv()

            for dq in (-1, 1):

                @pl.when((x == c) & inside(dq))
                def _(c=c, dq=dq):
                    side_copy(dq, c, True).start()

    for c in range(2):

        @pl.when(x == c)
        def _(c=c):
            local_copy(c, 0).wait()

    to_turns = wavenumber / (2.0 * math.pi)

    def scale_window(at):
        base = (r - 2).astype(jnp.float32)
        weight[0:1, at] = (geo[0:1, at] - base) * to_turns
        weight[1:2, at] = geo[1:2, at] * to_turns

    scale_window(slice(2 * B, 3 * B))
    weight[2:3, 2 * B : 3 * B] = geo[2:3, 2 * B : 3 * B]

    def spread_own(i, carry):
        cols = pl.ds(pl.multiple_of(2 * B + i * 128, 128), 128)
        at = pl.ds(pl.multiple_of(i * 128, 128), 128)
        for row, ref in ((0, own_x), (1, own_y), (2, own_a)):
            line = jnp.broadcast_to(weight[row : row + 1, cols], (128, 128))
            ref[at, :] = jnp.transpose(line)
        return carry

    lax.fori_loop(0, B // 128, spread_own, 0)

    def wait_geo():
        for c in range(2):
            for dq in (-1, 1):

                @pl.when((x == c) & inside(-dq))
                def _(c=c, dq=dq):
                    geo_copy(dq, c).wait_recv()

    def mask_weights():
        for slot in range(SLOTS):
            hit = jnp.float32(0.0)
            for s in range(SLOTS):
                found = (neighbours[s, r] == r + slot - 2) & (s < counts[r])
                hit = jnp.maximum(hit, jnp.where(found, jnp.float32(1.0), jnp.float32(0.0)))
            at = slice(slot * B, slot * B + B)
            scale_window(at)
            weight[2:3, at] = geo[2:3, at] * (hit * (0.5 / math.pi))

    tiny = 2.5e-10

    def evaluate(i):
        def one(g, carry, width=GROUP):
            cols = pl.ds(pl.multiple_of(g * width, width), width)
            col_x, col_y, col_a = weight[0:1, cols], weight[1:2, cols], weight[2:3, cols]
            for h in range(CHUNK // 128):
                at = pl.ds(pl.multiple_of(i * CHUNK + h * 128, 128), 128)
                for lane in range(width // 128):
                    part = slice(lane * 128, lane * 128 + 128)
                    dx = own_x[at, :] - col_x[:, part]
                    dy = own_y[at, :] - col_y[:, part]
                    square = jnp.maximum(dx * dx + dy * dy, tiny)
                    inv = lax.rsqrt(square)
                    turns = square * inv
                    f = turns - ((turns + MAGIC) - MAGIC)
                    z = f * f
                    poly = jnp.float32(SIN[5])
                    for coefficient in SIN[4::-1]:
                        poly = poly * z + coefficient
                    value = (poly * f) * inv * (own_a[at, :] * col_a[:, part])
                    lanes = pl.ds(pl.multiple_of(g * width + lane * 128, 128), 128)
                    tiles[at, lanes] = value.astype(jnp.bfloat16)
            return carry

        per_block = B // GROUP

        def outside(g, carry):
            return one(jnp.where(g < 2, g, g + 1), carry, B)

        lax.fori_loop(0, 4, outside, 0)
        lax.fori_loop(2 * per_block + i, 3 * per_block, one, 0)

        def mirror(g, carry):
            at = pl.ds(pl.multiple_of(i * CHUNK, CHUNK), CHUNK)
            rows = pl.ds(pl.multiple_of(g * CHUNK, CHUNK), CHUNK)
            to = pl.ds(pl.multiple_of(2 * B + g * CHUNK, CHUNK), CHUNK)
            cols = pl.ds(pl.multiple_of(2 * B + i * CHUNK, CHUNK), CHUNK)
            tiles[at, to] = jnp.transpose(tiles[rows, cols])
            return carry

        lax.fori_loop(0, i, mirror, 0)

    onward = 1 - 2 * x

    def first_copy(i, k):
        held = (2, 2, 2, 3 - 2 * x)[k]
        slot = (4, 0, 1 + 2 * x, 1 + 2 * x)[k]
        target = ((q - 1, x), (q + 1, x), (q, 1 - x), (q + onward, x))[k]
        rows = pl.ds(pl.multiple_of(held * B + i * CHUNK, CHUNK), CHUNK)
        to = pl.ds(pl.multiple_of(slot * B + i * CHUNK, CHUNK), CHUNK)
        return pltpu.make_async_remote_copy(
            src_ref=first.at[rows, :],
            dst_ref=first.at[to, :],
            send_sem=first_sem.at[0, k, i],
            recv_sem=first_sem.at[1, k, i],
            device_id=target,
            device_id_type=MESH,
        )

    def sends(k):
        return (q > 0, q < rows_n - 1, None, inside(onward))[k]

    def receives(k):
        return (q < rows_n - 1, q > 0, None, inside(-onward))[k]

    def guarded(condition, action):
        if condition is None:
            action()
        else:
            pl.when(condition)(action)

    def pass_first_on(i):
        first_copy(i, 2).wait_recv()
        guarded(sends(3), lambda: first_copy(i, 3).start())

    def product_and_send(i):
        at = pl.ds(pl.multiple_of(i * CHUNK, CHUNK), CHUNK)
        part = lax.dot_general(
            tiles[at, :],
            wide[...],
            (((1,), (1,)), ((), ())),
            preferred_element_type=jnp.float32,
        )
        rows = pl.ds(pl.multiple_of(2 * B + i * CHUNK, CHUNK), CHUNK)
        first[rows, :] = part.astype(jnp.bfloat16)
        for k in (2, 0, 1):
            guarded(sends(k), lambda k=k: first_copy(i, k).start())

    wait_geo()
    for copy in table_copies:
        copy.wait()
    mask_weights()
    chunks = B // CHUNK
    early = chunks - 1

    def eval_only(i, carry):
        evaluate(i)
        return carry

    lax.fori_loop(0, 1, eval_only, 0)
    pass_sketch_on()
    lax.fori_loop(1, early, eval_only, 0)

    for c in range(2):

        @pl.when(x == c)
        def _(c=c):
            local_copy(c, 1).wait()

        for dq in (-1, 1):

            @pl.when((x == c) & inside(-dq))
            def _(c=c, dq=dq):
                side_copy(dq, c, False).wait_recv()
                side_copy(dq, c, True).wait_recv()

    def product_only(i, carry):
        product_and_send(i)
        return carry

    lax.fori_loop(0, early, product_only, 0)

    def both(i, carry):
        evaluate(i)
        product_and_send(i)
        return carry

    lax.fori_loop(early, chunks, both, 0)

    def pass_chunk(i, carry):
        pass_first_on(i)
        return carry

    lax.fori_loop(0, chunks, pass_chunk, 0)

    def first_wait(i, carry):
        for k in range(4):
            if k != 2:
                guarded(receives(k), lambda k=k: first_copy(i, k).wait_recv())
            guarded(sends(k), lambda k=k: first_copy(i, k).wait_send())
        return carry

    lax.fori_loop(0, chunks, first_wait, 0)

    def second_product(i, carry):
        at = pl.ds(pl.multiple_of(i * CHUNK, CHUNK), CHUNK)
        to = pl.ds(pl.multiple_of(x * B + i * CHUNK, CHUNK), CHUNK)
        part = jnp.dot(tiles[at, :], first[...], preferred_element_type=jnp.float32)
        second[to, :] = part
        turned = jnp.transpose(part)
        product = jnp.dot(
            turned, part, precision=lax.Precision.HIGHEST, preferred_element_type=jnp.float32
        )
        gram_send[0] += product
        return carry

    gram_send[0] = jnp.zeros((128, 128), jnp.float32)
    lax.fori_loop(0, chunks, second_product, 0)

    half = pl.ds(pl.multiple_of(x * B, B), B)
    pair = pltpu.make_async_remote_copy(
        src_ref=second.at[half, :],
        dst_ref=second.at[half, :],
        send_sem=pair_sem.at[0],
        recv_sem=pair_sem.at[1],
        device_id=(q, 1 - x),
        device_id_type=MESH,
    )

    targets = [(q, 1 - x)] + [(partner_q(flip), x) for flip in flips]
    for k, target in enumerate(targets):
        copy = pltpu.make_async_remote_copy(
            src_ref=gram_send.at[k],
            dst_ref=gram_recv.at[k],
            send_sem=gram_sem.at[0, k],
            recv_sem=gram_sem.at[1, k],
            device_id=target,
            device_id_type=MESH,
        )
        copy.start()
        if k == 0:
            pair.start()
        copy.wait()
        total = gram_send[k] + gram_recv[k]
        if k + 1 < len(targets):
            gram_send[k + 1] = total
        else:
            gram[...] = total

    for c in range(2):
        for dq in (-1, 1):

            @pl.when((x == c) & inside(dq))
            def _(c=c, dq=dq):
                geo_copy(dq, c).wait_send()

    for c in range(2):

        @pl.when(x == c)
        def _(c=c):
            cross_copy(c).wait_send()

        for dq in (-1, 1):

            @pl.when((x == c) & inside(dq))
            def _(c=c, dq=dq):
                side_copy(dq, c, False).wait_send()
                side_copy(dq, c, True).wait_send()

    pair.wait()


def finish_kernel(scale, gram, second, modes, inverse):
    size = gram.shape[0]
    lane = lax.broadcasted_iota(jnp.int32, (8, size), 1)
    sub = lax.broadcasted_iota(jnp.int32, (8, size), 0)
    groups = [gram[8 * k : 8 * k + 8, :] for k in range(size // 8)]
    for j in range(size):
        own, inner = j // 8, j % 8
        line = groups[own][inner : inner + 1, :]
        root = lax.rsqrt(line[:, j : j + 1])
        line = jnp.where(lane[0:1] == j, 1.0, line) * root
        for k in range(own, size // 8):
            old = groups[k]
            column = old[:, j : j + 1] * root
            new = jnp.where(lane == j, 0.0, old) - column * line
            if k == own:
                new = jnp.where(sub > inner, new, jnp.where(sub == inner, line, old))
            groups[k] = new
    for k in range(size // 8):
        inverse[8 * k : 8 * k + 8, :] = jnp.where(lane <= sub + 8 * k, groups[k], 0.0) * scale
    start = pl.multiple_of(lax.axis_index("cols") * 64, 64)
    lower = inverse[pl.ds(start, 64), :]
    for i in range(4):
        at = slice(i * 512, i * 512 + 512)
        modes[:, at] = jnp.dot(
            lower,
            jnp.transpose(second[at, :]),
            precision=lax.Precision.HIGHEST,
            preferred_element_type=jnp.float32,
        )


def fast_body(sketch, geometry, neighbours, counts):
    rows_n = lax.axis_size("rows")
    wavenumber = 4.0 * math.sqrt(B)
    levels = 1 + rows_n.bit_length() - 1
    vmem = pl.BlockSpec(memory_space=pltpu.VMEM)
    hbm = pl.BlockSpec(memory_space=pltpu.HBM)
    gram, second = pl.pallas_call(
        functools.partial(fast_kernel, rows_n, wavenumber),
        name="sketch_twice",
        out_shape=(
            jax.ShapeDtypeStruct((128, 128), jnp.float32),
            jax.ShapeDtypeStruct((2 * B, 128), jnp.float32),
        ),
        in_specs=[hbm, hbm, hbm, hbm],
        out_specs=(vmem, vmem),
        scratch_shapes=[
            pltpu.VMEM((B, SLOTS * B), jnp.bfloat16),
            pltpu.VMEM((128, SLOTS * B), jnp.bfloat16),
            pltpu.VMEM((3, SLOTS * B), jnp.float32),
            pltpu.VMEM((3, SLOTS * B), jnp.float32),
            pltpu.VMEM((SLOTS * B, 128), jnp.bfloat16),
            pltpu.VMEM((B, 128), jnp.float32),
            pltpu.VMEM((B, 128), jnp.float32),
            pltpu.VMEM((B, 128), jnp.float32),
            pltpu.VMEM((levels, 128, 128), jnp.float32),
            pltpu.VMEM((levels, 128, 128), jnp.float32),
            pltpu.SemaphoreType.DMA((2, 2)),
            pltpu.SemaphoreType.DMA((2, 6)),
            pltpu.SemaphoreType.DMA((2, 4, B // CHUNK)),
            pltpu.SemaphoreType.DMA((2, levels)),
            pltpu.SemaphoreType.DMA((2,)),
            pltpu.SemaphoreType.DMA((4,)),
            pltpu.SMEM((SLOTS, 2 * rows_n), jnp.int32),
            pltpu.SMEM((2 * rows_n,), jnp.int32),
        ],
        compiler_params=pltpu.CompilerParams(
            collective_id=0, has_side_effects=True, vmem_limit_bytes=48 * 1024 * 1024
        ),
    )(sketch, geometry, jnp.transpose(neighbours), counts)
    scale = math.sqrt(2 * B * rows_n)
    return pl.pallas_call(
        functools.partial(finish_kernel, scale),
        name="orthonormal_rows",
        out_shape=jax.ShapeDtypeStruct((64, 2 * B), jnp.float32),
        in_specs=[vmem, vmem],
        out_specs=vmem,
        scratch_shapes=[pltpu.VMEM((128, 128), jnp.float32)],
        compiler_params=pltpu.CompilerParams(vmem_limit_bytes=16 * 1024 * 1024),
    )(gram, second)


def solution(mesh):
    rows_n, cols_n = mesh.shape["rows"], mesh.shape["cols"]
    pair = cols_n == 2 and rows_n & (rows_n - 1) == 0
    return jax.shard_map(
        fast_body if pair else body,
        mesh=mesh,
        in_specs=(P("cols", "rows"), P(None, "rows"), P(), P()),
        out_specs=P("cols", "rows"),
        check_vma=False,
    )
```

```python
import functools
import math

import jax
import jax.numpy as jnp
from jax import lax
from jax.experimental import pallas as pl
from jax.experimental.pallas import tpu as pltpu
from jax.sharding import PartitionSpec as P

B = 1024
BLK_DEV = 2


highest = lax.Precision.HIGHEST


def padded(shard, sides, width):
    for axis, dim in sides:
        size, length = (lax.axis_size(axis), shard.shape[dim])
        up = [(i, (i + 1) % size) for i in range(size - 1)]
        down = [(j, i) for i, j in up]
        last = lax.slice_in_dim(shard, length - width, length, axis=dim)
        initial = lax.slice_in_dim(shard, 0, width, axis=dim)
        before = lax.ppermute(last, axis, up)
        after = lax.ppermute(initial, axis, down)
        shard = jnp.concatenate([before, shard, after], axis=dim)
    return shard


def spread(value, axis, source):
    kept = jnp.where(lax.axis_index(axis) == source, value, 0).astype(value.dtype)
    return lax.psum(kept, axis)


def kernel_tile(col_geo, row_geo, wavenumber):
    delta_x = col_geo[0][:, None] - row_geo[0][None, :]
    delta_y = col_geo[1][:, None] - row_geo[1][None, :]
    distance = jnp.sqrt(delta_x * delta_x + delta_y * delta_y)
    weights = col_geo[2][:, None] * row_geo[2][None, :]
    return (weights * jnp.sinc(distance * (wavenumber / math.pi))).astype(jnp.bfloat16)


def choose_slice(own_array, start, width):
    own_part = lax.dynamic_slice_in_dim(own_array, start, width, 1)
    return own_part


def task_lists(neighbours, counts, device_index, unit_blocks):
    slot_count = neighbours.shape[1]
    unit_count = unit_blocks.shape[0]
    slot_ids = jnp.arange(slot_count, dtype=jnp.int32)
    owners = jnp.zeros((unit_count,), jnp.int32) + device_index
    row_blocks = owners * BLK_DEV + unit_blocks
    flags = (slot_ids[None, :] < counts[row_blocks][:, None]).astype(jnp.int32).reshape(-1)
    column_ids = neighbours[row_blocks].reshape(-1)
    base_blocks = jnp.repeat(owners * BLK_DEV - BLK_DEV, slot_count)
    starts = (column_ids - base_blocks) * B
    task_total = flags.shape[0]
    task_ids = jnp.arange(task_total, dtype=jnp.int32)
    rank = jnp.cumsum(flags) - flags
    taken = flags == 1
    task_sides = jnp.zeros((task_total,), jnp.int32)
    target = jnp.where(taken, rank, task_total)
    blank = jnp.zeros((task_total + 1,), jnp.int32)
    order_side = blank.at[target].set(task_sides)
    order_unit = blank.at[target].set(task_ids // slot_count % unit_count)
    order_start = blank.at[target].set(starts)
    return (order_side, order_unit, order_start, jnp.sum(taken.astype(jnp.int32)))


def evaluate_tiles(tables, geo_wide, unit_blocks, unit_offset, unit_rows, capacity, wavenumber):
    order_side, order_unit, order_start, own_count = tables

    def add_tile(task, stored):
        row_start = (BLK_DEV + unit_blocks[order_unit[task]]) * B + unit_offset
        row_geo = choose_slice(geo_wide, row_start, unit_rows)
        col_geo = choose_slice(geo_wide, order_start[task], B)
        tile = kernel_tile(col_geo, row_geo, wavenumber)
        return lax.dynamic_update_slice(stored, tile[None], (task, 0, 0))

    initial = jnp.zeros((capacity, B, unit_rows), jnp.bfloat16)
    return lax.fori_loop(0, own_count, add_tile, initial)


def apply_tiles(stored, tables, panel_wide, unit_rows, unit_count):
    order_side, order_unit, order_start, own_count = tables
    columns = panel_wide.shape[0]
    side_count = 1

    def add_term(task, running):
        col_panel = choose_slice(panel_wide, order_start[task], B)
        term = jnp.dot(col_panel, stored[task], preferred_element_type=jnp.float32)
        return running + term[None]

    initial = jnp.zeros((side_count, columns, unit_count * unit_rows), jnp.float32)
    return lax.fori_loop(0, own_count, add_term, initial)


def operator_product(panel_t, stored, tables, unit_rows, unit_count):
    panel_wide = padded(panel_t, (("rows", 1),), BLK_DEV * B)
    gathered = apply_tiles(
        stored,
        tables,
        lax.all_gather(panel_wide, "cols", axis=0, tiled=True),
        unit_rows,
        unit_count,
    )[0]
    return lax.all_to_all(gathered, "cols", split_axis=0, concat_axis=1, tiled=True)


def normalize(current):
    gram_matrix = lax.psum(jnp.dot(current, current.T, precision=highest), "rows")
    cholesky_factor = jnp.linalg.cholesky(gram_matrix)
    return lax.linalg.triangular_solve(cholesky_factor, current, left_side=True, lower=True)


def orthonormal(second_product):
    position = lax.axis_index("cols")
    panels = lax.axis_size("cols")
    norm_scale = math.sqrt(second_product.shape[1] * lax.axis_size("rows"))
    mode_rows = jnp.zeros_like(second_product)
    removed = jnp.zeros_like(second_product)
    for panel_index in range(panels):
        basis_rows = normalize(second_product - removed)
        mode_rows = jnp.where(position == panel_index, basis_rows, mode_rows)
        if panel_index + 1 < panels:
            finished = spread(basis_rows, "cols", panel_index)
            coefficients = lax.psum(jnp.dot(finished, second_product.T, precision=highest), "rows")
            update = jnp.dot(coefficients.T, finished, precision=highest)
            removed = removed + jnp.where(position > panel_index, update, 0.0)
    return mode_rows * norm_scale


def body(sketch, geometry, neighbours, counts):
    wavenumber = 4.0 * math.sqrt(B)
    device_index = lax.axis_index("rows")
    geo_wide = padded(geometry, (("rows", 1),), BLK_DEV * B)
    unit_blocks = jnp.arange(BLK_DEV, dtype=jnp.int32)
    unit_offset = 0
    unit_rows = BLK_DEV * B // lax.axis_size("cols")
    slice_start = lax.axis_index("cols") * unit_rows
    unit_blocks = jnp.reshape(slice_start // B, (1,))
    unit_offset = slice_start % B
    unit_count = unit_blocks.shape[0]
    tables = task_lists(neighbours, counts, device_index, unit_blocks)
    capacity = unit_count * neighbours.shape[1]
    stored = evaluate_tiles(
        tables, geo_wide, unit_blocks, unit_offset, unit_rows, capacity, wavenumber
    )
    first_product = operator_product(sketch, stored, tables, unit_rows, unit_count).astype(
        jnp.bfloat16
    )
    second_product = operator_product(first_product, stored, tables, unit_rows, unit_count)
    return orthonormal(second_product)


MESH = pl.DeviceIdType.MESH
SLOTS = 5
CHUNK = 256
GROUP = 256
SIN = (
    6.28318330620465,
    -41.34144799998349,
    81.59666336606338,
    -76.58390226519525,
    41.21913554078422,
    -12.289783804974757,
)
MAGIC = 12582912.0


def column_range(dq, to_col):
    first = -2 * dq - to_col + 2
    kept = [e for e in range(2) if 0 <= first + e < SLOTS]
    lo, count = kept[0], len(kept)
    return (first + lo) * B, lo * B, count * B


def fast_kernel(
    rows_n,
    wavenumber,
    sketch,
    geometry,
    neighbours_hbm,
    counts_hbm,
    gram,
    second,
    tiles,
    wide,
    geo,
    weight,
    first,
    own_x,
    own_y,
    own_a,
    gram_sum,
    gram_send,
    gram_recv,
    geo_sem,
    sk_sem,
    first_sem,
    gram_sem,
    pair_sem,
    local_sem,
    neighbours,
    counts,
):
    q = lax.axis_index("rows")
    x = lax.axis_index("cols")
    r = 2 * q + x
    blocks_n = 2 * rows_n
    flips = [1 << k for k in range(rows_n.bit_length() - 1)]

    def partner_q(flip):
        return q + flip - 2 * flip * ((q // flip) % 2)

    barrier = pltpu.get_barrier_semaphore()
    pl.semaphore_signal(barrier, inc=1, device_id=(q, 1 - x), device_id_type=MESH)
    for flip in flips[1:]:
        pl.semaphore_signal(barrier, inc=1, device_id=(partner_q(flip), x), device_id_type=MESH)
    for dq in (-1, 1):

        @pl.when((q + dq >= 0) & (q + dq < rows_n))
        def _(dq=dq):
            pl.semaphore_signal(barrier, inc=1, device_id=(q + dq, x), device_id_type=MESH)

    def local_copy(c, k):
        at = column_range(0, c)[0]
        if k == 0:
            return pltpu.make_async_copy(geometry, geo.at[:, at : at + 2 * B], local_sem.at[0])
        held = wide.at[64 * c : 64 * c + 64, at : at + 2 * B]
        return pltpu.make_async_copy(sketch, held, local_sem.at[1])

    table_copies = (
        pltpu.make_async_copy(neighbours_hbm, neighbours, local_sem.at[2]),
        pltpu.make_async_copy(counts_hbm, counts, local_sem.at[3]),
    )
    for copy in table_copies:
        copy.start()
    for c in range(2):

        @pl.when(x == c)
        def _(c=c):
            local_copy(c, 0).start()
            local_copy(c, 1).start()

    for step in (-2, -1, 1, 2):

        @pl.when((r + step < 0) | (r + step >= blocks_n))
        def _(step=step):
            at = (2 + step) * B
            geo[:, at : at + B] = jnp.full((3, B), -1.0, jnp.float32)
            wide[:, at : at + B] = jnp.zeros((128, B), jnp.bfloat16)
            first[at : at + B, :] = jnp.zeros((B, 128), jnp.bfloat16)

    sides = jnp.where(q > 0, 1, 0) + jnp.where(q < rows_n - 1, 1, 0)
    pl.semaphore_wait(barrier, len(flips) + sides)

    def geo_copy(dq, col):
        to, lo, n = column_range(dq, col)
        k = (dq + 1) // 2
        return pltpu.make_async_remote_copy(
            src_ref=geometry.at[:, lo : lo + n],
            dst_ref=geo.at[:, to : to + n],
            send_sem=geo_sem.at[0, k],
            recv_sem=geo_sem.at[1, k],
            device_id=(q + dq, x),
            device_id_type=MESH,
        )

    def cross_copy(c):
        at = column_range(0, 1 - c)[0]
        return pltpu.make_async_remote_copy(
            src_ref=sketch,
            dst_ref=wide.at[64 * c : 64 * c + 64, at : at + 2 * B],
            send_sem=sk_sem.at[0, 0],
            recv_sem=sk_sem.at[1, 0],
            device_id=(q, 1 - c),
            device_id_type=MESH,
        )

    def side_copy(dq, c, passed_on):
        to, lo, n = column_range(dq, c)
        k = (1 if dq < 0 else 2) + (2 if passed_on else 0)
        panel = 1 - c if passed_on else c
        lines = slice(64 * panel, 64 * panel + 64)
        at = column_range(0, c)[0] + lo
        return pltpu.make_async_remote_copy(
            src_ref=wide.at[lines, at : at + n] if passed_on else sketch.at[:, lo : lo + n],
            dst_ref=wide.at[lines, to : to + n],
            send_sem=sk_sem.at[0, k],
            recv_sem=sk_sem.at[1, k],
            device_id=(q + dq, c),
            device_id_type=MESH,
        )

    def inside(dq):
        return (q + dq >= 0) & (q + dq < rows_n)

    for c in range(2):
        for dq in (-1, 1):

            @pl.when((x == c) & inside(dq))
            def _(c=c, dq=dq):
                geo_copy(dq, c).start()

    for c in range(2):

        @pl.when(x == c)
        def _(c=c):
            cross_copy(c).start()

        for dq in (-1, 1):

            @pl.when((x == c) & inside(dq))
            def _(c=c, dq=dq):
                side_copy(dq, c, False).start()

    def pass_sketch_on():
        for c in range(2):

            @pl.when(x == c)
            def _(c=c):
                cross_copy(1 - c).wait_recv()

            for dq in (-1, 1):

                @pl.when((x == c) & inside(dq))
                def _(c=c, dq=dq):
                    side_copy(dq, c, True).start()

    for c in range(2):

        @pl.when(x == c)
        def _(c=c):
            local_copy(c, 0).wait()

    to_turns = wavenumber / (2.0 * math.pi)

    def scale_window(at):
        base = (r - 2).astype(jnp.float32)
        weight[0:1, at] = (geo[0:1, at] - base) * to_turns
        weight[1:2, at] = geo[1:2, at] * to_turns

    scale_window(slice(2 * B, 3 * B))
    weight[2:3, 2 * B : 3 * B] = geo[2:3, 2 * B : 3 * B]

    def spread_own(i, carry):
        cols = pl.ds(pl.multiple_of(2 * B + i * 128, 128), 128)
        at = pl.ds(pl.multiple_of(i * 128, 128), 128)
        for row, ref in ((0, own_x), (1, own_y), (2, own_a)):
            line = jnp.broadcast_to(weight[row : row + 1, cols], (128, 128))
            ref[at, :] = jnp.transpose(line)
        return carry

    lax.fori_loop(0, B // 128, spread_own, 0)

    def wait_geo():
        for c in range(2):
            for dq in (-1, 1):

                @pl.when((x == c) & inside(-dq))
                def _(c=c, dq=dq):
                    geo_copy(dq, c).wait_recv()

    def mask_weights():
        for slot in range(SLOTS):
            hit = jnp.float32(0.0)
            for s in range(SLOTS):
                found = (neighbours[s, r] == r + slot - 2) & (s < counts[r])
                hit = jnp.maximum(hit, jnp.where(found, jnp.float32(1.0), jnp.float32(0.0)))
            at = slice(slot * B, slot * B + B)
            scale_window(at)
            weight[2:3, at] = geo[2:3, at] * (hit * (0.5 / math.pi))

    tiny = 2.5e-10

    def evaluate(i):
        def one(g, carry, width=GROUP):
            cols = pl.ds(pl.multiple_of(g * width, width), width)
            col_x, col_y, col_a = weight[0:1, cols], weight[1:2, cols], weight[2:3, cols]
            for h in range(CHUNK // 128):
                at = pl.ds(pl.multiple_of(i * CHUNK + h * 128, 128), 128)
                for lane in range(width // 128):
                    part = slice(lane * 128, lane * 128 + 128)
                    dx = own_x[at, :] - col_x[:, part]
                    dy = own_y[at, :] - col_y[:, part]
                    square = jnp.maximum(dx * dx + dy * dy, tiny)
                    inv = lax.rsqrt(square)
                    turns = square * inv
                    f = turns - ((turns + MAGIC) - MAGIC)
                    z = f * f
                    poly = jnp.float32(SIN[5])
                    for coefficient in SIN[4::-1]:
                        poly = poly * z + coefficient
                    value = (poly * f) * inv * (own_a[at, :] * col_a[:, part])
                    lanes = pl.ds(pl.multiple_of(g * width + lane * 128, 128), 128)
                    tiles[at, lanes] = value.astype(jnp.bfloat16)
            return carry

        per_block = B // GROUP

        def outside(g, carry):
            return one(jnp.where(g < 2, g, g + 1), carry, B)

        lax.fori_loop(0, 4, outside, 0)
        lax.fori_loop(2 * per_block + i, 3 * per_block, one, 0)

        def mirror(g, carry):
            at = pl.ds(pl.multiple_of(i * CHUNK, CHUNK), CHUNK)
            rows = pl.ds(pl.multiple_of(g * CHUNK, CHUNK), CHUNK)
            to = pl.ds(pl.multiple_of(2 * B + g * CHUNK, CHUNK), CHUNK)
            cols = pl.ds(pl.multiple_of(2 * B + i * CHUNK, CHUNK), CHUNK)
            tiles[at, to] = jnp.transpose(tiles[rows, cols])
            return carry

        lax.fori_loop(0, i, mirror, 0)

    onward = 1 - 2 * x

    def first_copy(i, k):
        held = (2, 2, 2, 3 - 2 * x)[k]
        slot = (4, 0, 1 + 2 * x, 1 + 2 * x)[k]
        target = ((q - 1, x), (q + 1, x), (q, 1 - x), (q + onward, x))[k]
        rows = pl.ds(pl.multiple_of(held * B + i * CHUNK, CHUNK), CHUNK)
        to = pl.ds(pl.multiple_of(slot * B + i * CHUNK, CHUNK), CHUNK)
        return pltpu.make_async_remote_copy(
            src_ref=first.at[rows, :],
            dst_ref=first.at[to, :],
            send_sem=first_sem.at[0, k, i],
            recv_sem=first_sem.at[1, k, i],
            device_id=target,
            device_id_type=MESH,
        )

    def sends(k):
        return (q > 0, q < rows_n - 1, None, inside(onward))[k]

    def receives(k):
        return (q < rows_n - 1, q > 0, None, inside(-onward))[k]

    def guarded(condition, action):
        if condition is None:
            action()
        else:
            pl.when(condition)(action)

    def pass_first_on(i):
        first_copy(i, 2).wait_recv()
        guarded(sends(3), lambda: first_copy(i, 3).start())

    def product_and_send(i):
        at = pl.ds(pl.multiple_of(i * CHUNK, CHUNK), CHUNK)
        part = lax.dot_general(
            tiles[at, :],
            wide[...],
            (((1,), (1,)), ((), ())),
            preferred_element_type=jnp.float32,
        )
        rows = pl.ds(pl.multiple_of(2 * B + i * CHUNK, CHUNK), CHUNK)
        first[rows, :] = part.astype(jnp.bfloat16)
        for k in (2, 0, 1):
            guarded(sends(k), lambda k=k: first_copy(i, k).start())

    wait_geo()
    for copy in table_copies:
        copy.wait()
    mask_weights()
    chunks = B // CHUNK
    early = chunks - 1

    def eval_only(i, carry):
        evaluate(i)
        return carry

    lax.fori_loop(0, 1, eval_only, 0)
    pass_sketch_on()
    lax.fori_loop(1, early, eval_only, 0)

    for c in range(2):

        @pl.when(x == c)
        def _(c=c):
            local_copy(c, 1).wait()

        for dq in (-1, 1):

            @pl.when((x == c) & inside(-dq))
            def _(c=c, dq=dq):
                side_copy(dq, c, False).wait_recv()
                side_copy(dq, c, True).wait_recv()

    def product_only(i, carry):
        product_and_send(i)
        return carry

    lax.fori_loop(0, early, product_only, 0)

    def both(i, carry):
        evaluate(i)
        product_and_send(i)
        return carry

    lax.fori_loop(early, chunks, both, 0)

    def pass_chunk(i, carry):
        pass_first_on(i)
        return carry

    lax.fori_loop(0, chunks, pass_chunk, 0)

    def first_wait(i, carry):
        for k in range(4):
            if k != 2:
                guarded(receives(k), lambda k=k: first_copy(i, k).wait_recv())
            guarded(sends(k), lambda k=k: first_copy(i, k).wait_send())
        return carry

    lax.fori_loop(0, chunks, first_wait, 0)

    def pair_copy(i):
        rows = pl.ds(pl.multiple_of(x * B + i * CHUNK, CHUNK), CHUNK)
        return pltpu.make_async_remote_copy(
            src_ref=second.at[rows, :],
            dst_ref=second.at[rows, :],
            send_sem=pair_sem.at[0, i],
            recv_sem=pair_sem.at[1, i],
            device_id=(q, 1 - x),
            device_id_type=MESH,
        )

    def second_product(i, carry):
        at = pl.ds(pl.multiple_of(i * CHUNK, CHUNK), CHUNK)
        to = pl.ds(pl.multiple_of(x * B + i * CHUNK, CHUNK), CHUNK)
        part = jnp.dot(tiles[at, :], first[...], preferred_element_type=jnp.float32)
        second[to, :] = part
        pair_copy(i).start()
        turned = jnp.transpose(part)
        product = jnp.dot(
            turned, part, precision=lax.Precision.HIGHEST, preferred_element_type=jnp.float32
        )
        gram_sum[...] += product
        return carry

    gram_sum[...] = jnp.zeros((128, 128), jnp.float32)
    lax.fori_loop(0, chunks, second_product, 0)

    def exchange(src, dst, k, target):
        copy = pltpu.make_async_remote_copy(
            src_ref=src,
            dst_ref=dst,
            send_sem=gram_sem.at[0, k],
            recv_sem=gram_sem.at[1, k],
            device_id=target,
            device_id_type=MESH,
        )
        copy.start()
        copy.wait()

    mine = pl.ds(pl.multiple_of((q % 2) * 64, 64), 64)
    theirs = pl.ds(pl.multiple_of((1 - q % 2) * 64, 64), 64)
    exchange(gram_sum.at[theirs, :], gram_recv.at[0], 0, (partner_q(1), x))
    gram_send[0] = gram_sum[mine, :] + gram_recv[0]
    targets = [(partner_q(flip), x) for flip in flips[1:]] + [(q, 1 - x)]
    for k, target in enumerate(targets):
        exchange(gram_send.at[k], gram_recv.at[k + 1], k + 1, target)
        gram_send[k + 1] = gram_send[k] + gram_recv[k + 1]
    last = len(targets)
    gram[mine, :] = gram_send[last]
    exchange(gram_send.at[last], gram.at[mine, :], last + 1, (partner_q(1), x))

    for c in range(2):
        for dq in (-1, 1):

            @pl.when((x == c) & inside(dq))
            def _(c=c, dq=dq):
                geo_copy(dq, c).wait_send()

    for c in range(2):

        @pl.when(x == c)
        def _(c=c):
            cross_copy(c).wait_send()

        for dq in (-1, 1):

            @pl.when((x == c) & inside(dq))
            def _(c=c, dq=dq):
                side_copy(dq, c, False).wait_send()
                side_copy(dq, c, True).wait_send()

    def pair_wait(i, carry):
        pair_copy(i).wait()
        return carry

    lax.fori_loop(0, chunks, pair_wait, 0)


def finish_kernel(scale, gram, second, modes, inverse):
    size = gram.shape[0]
    lane = lax.broadcasted_iota(jnp.int32, (8, size), 1)
    sub = lax.broadcasted_iota(jnp.int32, (8, size), 0)
    groups = [gram[8 * k : 8 * k + 8, :] for k in range(size // 8)]
    for j in range(size):
        own, inner = j // 8, j % 8
        line = groups[own][inner : inner + 1, :]
        root = lax.rsqrt(line[:, j : j + 1])
        line = jnp.where(lane[0:1] == j, 1.0, line) * root
        for k in range(own, size // 8):
            old = groups[k]
            column = old[:, j : j + 1] * root
            new = jnp.where(lane == j, 0.0, old) - column * line
            if k == own:
                new = jnp.where(sub > inner, new, jnp.where(sub == inner, line, old))
            groups[k] = new
    for k in range(size // 8):
        inverse[8 * k : 8 * k + 8, :] = jnp.where(lane <= sub + 8 * k, groups[k], 0.0) * scale
    start = pl.multiple_of(lax.axis_index("cols") * 64, 64)
    lower = inverse[pl.ds(start, 64), :]
    for i in range(4):
        at = slice(i * 512, i * 512 + 512)
        modes[:, at] = jnp.dot(
            lower,
            jnp.transpose(second[at, :]),
            precision=lax.Precision.HIGHEST,
            preferred_element_type=jnp.float32,
        )


def fast_body(sketch, geometry, neighbours, counts):
    rows_n = lax.axis_size("rows")
    wavenumber = 4.0 * math.sqrt(B)
    levels = 1 + rows_n.bit_length() - 1
    vmem = pl.BlockSpec(memory_space=pltpu.VMEM)
    hbm = pl.BlockSpec(memory_space=pltpu.HBM)
    gram, second = pl.pallas_call(
        functools.partial(fast_kernel, rows_n, wavenumber),
        name="sketch_twice",
        out_shape=(
            jax.ShapeDtypeStruct((128, 128), jnp.float32),
            jax.ShapeDtypeStruct((2 * B, 128), jnp.float32),
        ),
        in_specs=[hbm, hbm, hbm, hbm],
        out_specs=(vmem, vmem),
        scratch_shapes=[
            pltpu.VMEM((B, SLOTS * B), jnp.bfloat16),
            pltpu.VMEM((128, SLOTS * B), jnp.bfloat16),
            pltpu.VMEM((3, SLOTS * B), jnp.float32),
            pltpu.VMEM((3, SLOTS * B), jnp.float32),
            pltpu.VMEM((SLOTS * B, 128), jnp.bfloat16),
            pltpu.VMEM((B, 128), jnp.float32),
            pltpu.VMEM((B, 128), jnp.float32),
            pltpu.VMEM((B, 128), jnp.float32),
            pltpu.VMEM((128, 128), jnp.float32),
            pltpu.VMEM((levels, 64, 128), jnp.float32),
            pltpu.VMEM((levels, 64, 128), jnp.float32),
            pltpu.SemaphoreType.DMA((2, 2)),
            pltpu.SemaphoreType.DMA((2, 6)),
            pltpu.SemaphoreType.DMA((2, 4, B // CHUNK)),
            pltpu.SemaphoreType.DMA((2, levels + 1)),
            pltpu.SemaphoreType.DMA((2, B // CHUNK)),
            pltpu.SemaphoreType.DMA((4,)),
            pltpu.SMEM((SLOTS, 2 * rows_n), jnp.int32),
            pltpu.SMEM((2 * rows_n,), jnp.int32),
        ],
        compiler_params=pltpu.CompilerParams(
            collective_id=0, has_side_effects=True, vmem_limit_bytes=48 * 1024 * 1024
        ),
    )(sketch, geometry, jnp.transpose(neighbours), counts)
    scale = math.sqrt(2 * B * rows_n)
    return pl.pallas_call(
        functools.partial(finish_kernel, scale),
        name="orthonormal_rows",
        out_shape=jax.ShapeDtypeStruct((64, 2 * B), jnp.float32),
        in_specs=[vmem, vmem],
        out_specs=vmem,
        scratch_shapes=[pltpu.VMEM((128, 128), jnp.float32)],
        compiler_params=pltpu.CompilerParams(vmem_limit_bytes=16 * 1024 * 1024),
    )(gram, second)


def solution(mesh):
    rows_n, cols_n = mesh.shape["rows"], mesh.shape["cols"]
    pair = cols_n == 2 and rows_n > 1 and rows_n & (rows_n - 1) == 0
    return jax.shard_map(
        fast_body if pair else body,
        mesh=mesh,
        in_specs=(P("cols", "rows"), P(None, "rows"), P(), P()),
        out_specs=P("cols", "rows"),
        check_vma=False,
    )
```

```python
import functools
import math

import jax
import jax.numpy as jnp
from jax import lax
from jax.experimental import pallas as pl
from jax.experimental.pallas import tpu as pltpu
from jax.sharding import PartitionSpec as P

B = 1024
BLK_DEV = 2


highest = lax.Precision.HIGHEST


def padded(shard, sides, width):
    for axis, dim in sides:
        size, length = (lax.axis_size(axis), shard.shape[dim])
        up = [(i, (i + 1) % size) for i in range(size - 1)]
        down = [(j, i) for i, j in up]
        last = lax.slice_in_dim(shard, length - width, length, axis=dim)
        initial = lax.slice_in_dim(shard, 0, width, axis=dim)
        before = lax.ppermute(last, axis, up)
        after = lax.ppermute(initial, axis, down)
        shard = jnp.concatenate([before, shard, after], axis=dim)
    return shard


def spread(value, axis, source):
    kept = jnp.where(lax.axis_index(axis) == source, value, 0).astype(value.dtype)
    return lax.psum(kept, axis)


def kernel_tile(col_geo, row_geo, wavenumber):
    delta_x = col_geo[0][:, None] - row_geo[0][None, :]
    delta_y = col_geo[1][:, None] - row_geo[1][None, :]
    distance = jnp.sqrt(delta_x * delta_x + delta_y * delta_y)
    weights = col_geo[2][:, None] * row_geo[2][None, :]
    return (weights * jnp.sinc(distance * (wavenumber / math.pi))).astype(jnp.bfloat16)


def choose_slice(own_array, start, width):
    own_part = lax.dynamic_slice_in_dim(own_array, start, width, 1)
    return own_part


def task_lists(neighbours, counts, device_index, unit_blocks):
    slot_count = neighbours.shape[1]
    unit_count = unit_blocks.shape[0]
    slot_ids = jnp.arange(slot_count, dtype=jnp.int32)
    owners = jnp.zeros((unit_count,), jnp.int32) + device_index
    row_blocks = owners * BLK_DEV + unit_blocks
    flags = (slot_ids[None, :] < counts[row_blocks][:, None]).astype(jnp.int32).reshape(-1)
    column_ids = neighbours[row_blocks].reshape(-1)
    base_blocks = jnp.repeat(owners * BLK_DEV - BLK_DEV, slot_count)
    starts = (column_ids - base_blocks) * B
    task_total = flags.shape[0]
    task_ids = jnp.arange(task_total, dtype=jnp.int32)
    rank = jnp.cumsum(flags) - flags
    taken = flags == 1
    task_sides = jnp.zeros((task_total,), jnp.int32)
    target = jnp.where(taken, rank, task_total)
    blank = jnp.zeros((task_total + 1,), jnp.int32)
    order_side = blank.at[target].set(task_sides)
    order_unit = blank.at[target].set(task_ids // slot_count % unit_count)
    order_start = blank.at[target].set(starts)
    return (order_side, order_unit, order_start, jnp.sum(taken.astype(jnp.int32)))


def evaluate_tiles(tables, geo_wide, unit_blocks, unit_offset, unit_rows, capacity, wavenumber):
    order_side, order_unit, order_start, own_count = tables

    def add_tile(task, stored):
        row_start = (BLK_DEV + unit_blocks[order_unit[task]]) * B + unit_offset
        row_geo = choose_slice(geo_wide, row_start, unit_rows)
        col_geo = choose_slice(geo_wide, order_start[task], B)
        tile = kernel_tile(col_geo, row_geo, wavenumber)
        return lax.dynamic_update_slice(stored, tile[None], (task, 0, 0))

    initial = jnp.zeros((capacity, B, unit_rows), jnp.bfloat16)
    return lax.fori_loop(0, own_count, add_tile, initial)


def apply_tiles(stored, tables, panel_wide, unit_rows, unit_count):
    order_side, order_unit, order_start, own_count = tables
    columns = panel_wide.shape[0]
    side_count = 1

    def add_term(task, running):
        col_panel = choose_slice(panel_wide, order_start[task], B)
        term = jnp.dot(col_panel, stored[task], preferred_element_type=jnp.float32)
        return running + term[None]

    initial = jnp.zeros((side_count, columns, unit_count * unit_rows), jnp.float32)
    return lax.fori_loop(0, own_count, add_term, initial)


def operator_product(panel_t, stored, tables, unit_rows, unit_count):
    panel_wide = padded(panel_t, (("rows", 1),), BLK_DEV * B)
    gathered = apply_tiles(
        stored,
        tables,
        lax.all_gather(panel_wide, "cols", axis=0, tiled=True),
        unit_rows,
        unit_count,
    )[0]
    return lax.all_to_all(gathered, "cols", split_axis=0, concat_axis=1, tiled=True)


def normalize(current):
    gram_matrix = lax.psum(jnp.dot(current, current.T, precision=highest), "rows")
    cholesky_factor = jnp.linalg.cholesky(gram_matrix)
    return lax.linalg.triangular_solve(cholesky_factor, current, left_side=True, lower=True)


def orthonormal(second_product):
    position = lax.axis_index("cols")
    panels = lax.axis_size("cols")
    norm_scale = math.sqrt(second_product.shape[1] * lax.axis_size("rows"))
    mode_rows = jnp.zeros_like(second_product)
    removed = jnp.zeros_like(second_product)
    for panel_index in range(panels):
        basis_rows = normalize(second_product - removed)
        mode_rows = jnp.where(position == panel_index, basis_rows, mode_rows)
        if panel_index + 1 < panels:
            finished = spread(basis_rows, "cols", panel_index)
            coefficients = lax.psum(jnp.dot(finished, second_product.T, precision=highest), "rows")
            update = jnp.dot(coefficients.T, finished, precision=highest)
            removed = removed + jnp.where(position > panel_index, update, 0.0)
    return mode_rows * norm_scale


def body(sketch, geometry, neighbours, counts):
    wavenumber = 4.0 * math.sqrt(B)
    device_index = lax.axis_index("rows")
    geo_wide = padded(geometry, (("rows", 1),), BLK_DEV * B)
    unit_blocks = jnp.arange(BLK_DEV, dtype=jnp.int32)
    unit_offset = 0
    unit_rows = BLK_DEV * B // lax.axis_size("cols")
    slice_start = lax.axis_index("cols") * unit_rows
    unit_blocks = jnp.reshape(slice_start // B, (1,))
    unit_offset = slice_start % B
    unit_count = unit_blocks.shape[0]
    tables = task_lists(neighbours, counts, device_index, unit_blocks)
    capacity = unit_count * neighbours.shape[1]
    stored = evaluate_tiles(
        tables, geo_wide, unit_blocks, unit_offset, unit_rows, capacity, wavenumber
    )
    first_product = operator_product(sketch, stored, tables, unit_rows, unit_count).astype(
        jnp.bfloat16
    )
    second_product = operator_product(first_product, stored, tables, unit_rows, unit_count)
    return orthonormal(second_product)


MESH = pl.DeviceIdType.MESH
SLOTS = 5
CHUNK = 256
GROUP = 256
SIN = (
    6.28318330620465,
    -41.34144799998349,
    81.59666336606338,
    -76.58390226519525,
    41.21913554078422,
    -12.289783804974757,
)
MAGIC = 12582912.0


def column_range(dq, to_col):
    first = -2 * dq - to_col + 2
    kept = [e for e in range(2) if 0 <= first + e < SLOTS]
    lo, count = kept[0], len(kept)
    return (first + lo) * B, lo * B, count * B


def fast_kernel(
    rows_n,
    wavenumber,
    sketch,
    geometry,
    neighbours_hbm,
    counts_hbm,
    gram,
    second,
    tiles,
    wide,
    geo,
    weight,
    first,
    own_x,
    own_y,
    own_a,
    gram_sum,
    gram_send,
    gram_recv,
    geo_sem,
    sk_sem,
    first_sem,
    gram_sem,
    pair_sem,
    local_sem,
    neighbours,
    counts,
):
    q = lax.axis_index("rows")
    x = lax.axis_index("cols")
    r = 2 * q + x
    blocks_n = 2 * rows_n
    flips = [1 << k for k in range(rows_n.bit_length() - 1)]

    def partner_q(flip):
        return q + flip - 2 * flip * ((q // flip) % 2)

    barrier = pltpu.get_barrier_semaphore()
    pl.semaphore_signal(barrier, inc=1, device_id=(q, 1 - x), device_id_type=MESH)
    for flip in flips[1:]:
        pl.semaphore_signal(barrier, inc=1, device_id=(partner_q(flip), x), device_id_type=MESH)
    for dq in (-1, 1):

        @pl.when((q + dq >= 0) & (q + dq < rows_n))
        def _(dq=dq):
            pl.semaphore_signal(barrier, inc=1, device_id=(q + dq, x), device_id_type=MESH)

    def local_copy(c, k):
        at = column_range(0, c)[0]
        if k == 0:
            return pltpu.make_async_copy(geometry, geo.at[:, at : at + 2 * B], local_sem.at[0])
        held = wide.at[64 * c : 64 * c + 64, at : at + 2 * B]
        return pltpu.make_async_copy(sketch, held, local_sem.at[1])

    table_copies = (
        pltpu.make_async_copy(neighbours_hbm, neighbours, local_sem.at[2]),
        pltpu.make_async_copy(counts_hbm, counts, local_sem.at[3]),
    )
    for copy in table_copies:
        copy.start()
    for c in range(2):

        @pl.when(x == c)
        def _(c=c):
            local_copy(c, 0).start()
            local_copy(c, 1).start()

    for step in (-2, -1, 1, 2):

        @pl.when((r + step < 0) | (r + step >= blocks_n))
        def _(step=step):
            at = (2 + step) * B
            geo[:, at : at + B] = jnp.full((3, B), -1.0, jnp.float32)
            wide[:, at : at + B] = jnp.zeros((128, B), jnp.bfloat16)
            first[at : at + B, :] = jnp.zeros((B, 128), jnp.bfloat16)

    sides = jnp.where(q > 0, 1, 0) + jnp.where(q < rows_n - 1, 1, 0)
    pl.semaphore_wait(barrier, len(flips) + sides)

    def geo_copy(dq, col):
        to, lo, n = column_range(dq, col)
        k = (dq + 1) // 2
        return pltpu.make_async_remote_copy(
            src_ref=geometry.at[:, lo : lo + n],
            dst_ref=geo.at[:, to : to + n],
            send_sem=geo_sem.at[0, k],
            recv_sem=geo_sem.at[1, k],
            device_id=(q + dq, x),
            device_id_type=MESH,
        )

    def cross_copy(c):
        at = column_range(0, 1 - c)[0]
        return pltpu.make_async_remote_copy(
            src_ref=sketch,
            dst_ref=wide.at[64 * c : 64 * c + 64, at : at + 2 * B],
            send_sem=sk_sem.at[0, 0],
            recv_sem=sk_sem.at[1, 0],
            device_id=(q, 1 - c),
            device_id_type=MESH,
        )

    def side_copy(dq, c, passed_on):
        to, lo, n = column_range(dq, c)
        k = (1 if dq < 0 else 2) + (2 if passed_on else 0)
        panel = 1 - c if passed_on else c
        lines = slice(64 * panel, 64 * panel + 64)
        at = column_range(0, c)[0] + lo
        return pltpu.make_async_remote_copy(
            src_ref=wide.at[lines, at : at + n] if passed_on else sketch.at[:, lo : lo + n],
            dst_ref=wide.at[lines, to : to + n],
            send_sem=sk_sem.at[0, k],
            recv_sem=sk_sem.at[1, k],
            device_id=(q + dq, c),
            device_id_type=MESH,
        )

    def inside(dq):
        return (q + dq >= 0) & (q + dq < rows_n)

    for c in range(2):
        for dq in (-1, 1):

            @pl.when((x == c) & inside(dq))
            def _(c=c, dq=dq):
                geo_copy(dq, c).start()

    for c in range(2):

        @pl.when(x == c)
        def _(c=c):
            cross_copy(c).start()

        for dq in (-1, 1):

            @pl.when((x == c) & inside(dq))
            def _(c=c, dq=dq):
                side_copy(dq, c, False).start()

    def pass_sketch_on():
        for c in range(2):

            @pl.when(x == c)
            def _(c=c):
                cross_copy(1 - c).wait_recv()

            for dq in (-1, 1):

                @pl.when((x == c) & inside(dq))
                def _(c=c, dq=dq):
                    side_copy(dq, c, True).start()

    for c in range(2):

        @pl.when(x == c)
        def _(c=c):
            local_copy(c, 0).wait()

    to_turns = wavenumber / (2.0 * math.pi)

    def scale_window(at):
        base = (r - 2).astype(jnp.float32)
        weight[0:1, at] = (geo[0:1, at] - base) * to_turns
        weight[1:2, at] = geo[1:2, at] * to_turns

    scale_window(slice(2 * B, 3 * B))
    weight[2:3, 2 * B : 3 * B] = geo[2:3, 2 * B : 3 * B]

    def spread_own(i, carry):
        cols = pl.ds(pl.multiple_of(2 * B + i * 128, 128), 128)
        at = pl.ds(pl.multiple_of(i * 128, 128), 128)
        for row, ref in ((0, own_x), (1, own_y), (2, own_a)):
            line = jnp.broadcast_to(weight[row : row + 1, cols], (128, 128))
            ref[at, :] = jnp.transpose(line)
        return carry

    lax.fori_loop(0, B // 128, spread_own, 0)

    def wait_geo():
        for c in range(2):
            for dq in (-1, 1):

                @pl.when((x == c) & inside(-dq))
                def _(c=c, dq=dq):
                    geo_copy(dq, c).wait_recv()

    def mask_weights():
        for slot in range(SLOTS):
            hit = jnp.float32(0.0)
            for s in range(SLOTS):
                found = (neighbours[s, r] == r + slot - 2) & (s < counts[r])
                hit = jnp.maximum(hit, jnp.where(found, jnp.float32(1.0), jnp.float32(0.0)))
            at = slice(slot * B, slot * B + B)
            scale_window(at)
            weight[2:3, at] = geo[2:3, at] * (hit * (0.5 / math.pi))

    tiny = 2.5e-10

    def evaluate(i):
        def one(g, carry, width=GROUP):
            cols = pl.ds(pl.multiple_of(g * width, width), width)
            col_x, col_y, col_a = weight[0:1, cols], weight[1:2, cols], weight[2:3, cols]
            for h in range(CHUNK // 128):
                at = pl.ds(pl.multiple_of(i * CHUNK + h * 128, 128), 128)
                for lane in range(width // 128):
                    part = slice(lane * 128, lane * 128 + 128)
                    dx = own_x[at, :] - col_x[:, part]
                    dy = own_y[at, :] - col_y[:, part]
                    square = jnp.maximum(dx * dx + dy * dy, tiny)
                    inv = lax.rsqrt(square)
                    turns = square * inv
                    f = turns - ((turns + MAGIC) - MAGIC)
                    z = f * f
                    poly = jnp.float32(SIN[5])
                    for coefficient in SIN[4::-1]:
                        poly = poly * z + coefficient
                    value = (poly * f) * inv * (own_a[at, :] * col_a[:, part])
                    lanes = pl.ds(pl.multiple_of(g * width + lane * 128, 128), 128)
                    tiles[at, lanes] = value.astype(jnp.bfloat16)
            return carry

        per_block = B // GROUP

        def outside(g, carry):
            return one(jnp.where(g < 2, g, g + 1), carry, B)

        lax.fori_loop(0, 4, outside, 0)
        lax.fori_loop(2 * per_block + i, 3 * per_block, one, 0)

        def mirror(g, carry):
            at = pl.ds(pl.multiple_of(i * CHUNK, CHUNK), CHUNK)
            rows = pl.ds(pl.multiple_of(g * CHUNK, CHUNK), CHUNK)
            to = pl.ds(pl.multiple_of(2 * B + g * CHUNK, CHUNK), CHUNK)
            cols = pl.ds(pl.multiple_of(2 * B + i * CHUNK, CHUNK), CHUNK)
            tiles[at, to] = jnp.transpose(tiles[rows, cols])
            return carry

        lax.fori_loop(0, i, mirror, 0)

    onward = 1 - 2 * x

    def first_copy(i, k):
        held = (2, 2, 2, 3 - 2 * x)[k]
        slot = (4, 0, 1 + 2 * x, 1 + 2 * x)[k]
        target = ((q - 1, x), (q + 1, x), (q, 1 - x), (q + onward, x))[k]
        rows = pl.ds(pl.multiple_of(held * B + i * CHUNK, CHUNK), CHUNK)
        to = pl.ds(pl.multiple_of(slot * B + i * CHUNK, CHUNK), CHUNK)
        return pltpu.make_async_remote_copy(
            src_ref=first.at[rows, :],
            dst_ref=first.at[to, :],
            send_sem=first_sem.at[0, k, i],
            recv_sem=first_sem.at[1, k, i],
            device_id=target,
            device_id_type=MESH,
        )

    def sends(k):
        return (q > 0, q < rows_n - 1, None, inside(onward))[k]

    def receives(k):
        return (q < rows_n - 1, q > 0, None, inside(-onward))[k]

    def guarded(condition, action):
        if condition is None:
            action()
        else:
            pl.when(condition)(action)

    def pass_first_on(i):
        first_copy(i, 2).wait_recv()
        guarded(sends(3), lambda: first_copy(i, 3).start())

    def product_and_send(i):
        at = pl.ds(pl.multiple_of(i * CHUNK, CHUNK), CHUNK)
        part = lax.dot_general(
            tiles[at, :],
            wide[...],
            (((1,), (1,)), ((), ())),
            preferred_element_type=jnp.float32,
        )
        rows = pl.ds(pl.multiple_of(2 * B + i * CHUNK, CHUNK), CHUNK)
        first[rows, :] = part.astype(jnp.bfloat16)
        for k in (2, 0, 1):
            guarded(sends(k), lambda k=k: first_copy(i, k).start())

    wait_geo()
    for copy in table_copies:
        copy.wait()
    mask_weights()
    chunks = B // CHUNK
    early = chunks - 1

    def eval_only(i, carry):
        evaluate(i)
        return carry

    lax.fori_loop(0, 1, eval_only, 0)
    pass_sketch_on()
    lax.fori_loop(1, early, eval_only, 0)

    for c in range(2):

        @pl.when(x == c)
        def _(c=c):
            local_copy(c, 1).wait()

        for dq in (-1, 1):

            @pl.when((x == c) & inside(-dq))
            def _(c=c, dq=dq):
                side_copy(dq, c, False).wait_recv()
                side_copy(dq, c, True).wait_recv()

    def product_only(i, carry):
        product_and_send(i)
        return carry

    lax.fori_loop(0, early, product_only, 0)

    def both(i, carry):
        evaluate(i)
        product_and_send(i)
        return carry

    lax.fori_loop(early, chunks, both, 0)

    def pass_chunk(i, carry):
        pass_first_on(i)
        return carry

    lax.fori_loop(0, chunks, pass_chunk, 0)

    def first_wait(i, carry):
        for k in range(4):
            if k != 2:
                guarded(receives(k), lambda k=k: first_copy(i, k).wait_recv())
            guarded(sends(k), lambda k=k: first_copy(i, k).wait_send())
        return carry

    lax.fori_loop(0, chunks, first_wait, 0)

    def pair_copy(i):
        rows = pl.ds(pl.multiple_of(x * B + i * CHUNK, CHUNK), CHUNK)
        return pltpu.make_async_remote_copy(
            src_ref=second.at[rows, :],
            dst_ref=second.at[rows, :],
            send_sem=pair_sem.at[0, i],
            recv_sem=pair_sem.at[1, i],
            device_id=(q, 1 - x),
            device_id_type=MESH,
        )

    def second_product(i, carry):
        at = pl.ds(pl.multiple_of(i * CHUNK, CHUNK), CHUNK)
        to = pl.ds(pl.multiple_of(x * B + i * CHUNK, CHUNK), CHUNK)
        part = jnp.dot(tiles[at, :], first[...], preferred_element_type=jnp.float32)
        second[to, :] = part
        pair_copy(i).start()
        turned = jnp.transpose(part)
        product = jnp.dot(
            turned, part, precision=lax.Precision.HIGHEST, preferred_element_type=jnp.float32
        )
        gram_sum[...] += product
        return carry

    gram_sum[...] = jnp.zeros((128, 128), jnp.float32)
    lax.fori_loop(0, chunks, second_product, 0)

    def exchange(src, dst, k, target):
        copy = pltpu.make_async_remote_copy(
            src_ref=src,
            dst_ref=dst,
            send_sem=gram_sem.at[0, k],
            recv_sem=gram_sem.at[1, k],
            device_id=target,
            device_id_type=MESH,
        )
        copy.start()
        copy.wait()

    mine = pl.ds(pl.multiple_of((q % 2) * 64, 64), 64)
    theirs = pl.ds(pl.multiple_of((1 - q % 2) * 64, 64), 64)
    exchange(gram_sum.at[theirs, :], gram_recv.at[0], 0, (partner_q(1), x))
    gram_send[0] = gram_sum[mine, :] + gram_recv[0]
    targets = [(partner_q(flip), x) for flip in flips[1:]] + [(q, 1 - x)]
    for k, target in enumerate(targets):
        exchange(gram_send.at[k], gram_recv.at[k + 1], k + 1, target)
        gram_send[k + 1] = gram_send[k] + gram_recv[k + 1]
    last = len(targets)
    gram[mine, :] = gram_send[last]
    exchange(gram_send.at[last], gram.at[mine, :], last + 1, (partner_q(1), x))

    for c in range(2):
        for dq in (-1, 1):

            @pl.when((x == c) & inside(dq))
            def _(c=c, dq=dq):
                geo_copy(dq, c).wait_send()

    for c in range(2):

        @pl.when(x == c)
        def _(c=c):
            cross_copy(c).wait_send()

        for dq in (-1, 1):

            @pl.when((x == c) & inside(dq))
            def _(c=c, dq=dq):
                side_copy(dq, c, False).wait_send()
                side_copy(dq, c, True).wait_send()

    def pair_wait(i, carry):
        pair_copy(i).wait()
        return carry

    lax.fori_loop(0, chunks, pair_wait, 0)


def finish_kernel(scale, gram, second, modes, inverse):
    size = gram.shape[0]
    lane = lax.broadcasted_iota(jnp.int32, (8, size), 1)
    sub = lax.broadcasted_iota(jnp.int32, (8, size), 0)
    groups = [gram[8 * k : 8 * k + 8, :] for k in range(size // 8)]
    whole = (8, size)
    for own in range(size // 8):
        base = 8 * own
        block = groups[own]
        column = [jnp.broadcast_to(block[:, base + c : base + c + 1], whole) for c in range(8)]
        roots, factor, lines = [], [], []
        for p in range(8):
            root = lax.rsqrt(jnp.broadcast_to(column[p][p : p + 1, :], whole))
            scaled = column[p] * root
            row = {}
            for c in range(p + 1, 8):
                row[c] = jnp.broadcast_to(column[c][p : p + 1, :], whole) * root
                column[c] = column[c] - scaled * row[c]
            line = jnp.broadcast_to(block[p : p + 1, :], whole)
            line = jnp.where(lane == base + p, 1.0, line) * root
            new = jnp.where(lane == base + p, 0.0, block) - scaled * line
            block = jnp.where(sub > p, new, block)
            roots.append(root)
            factor.append(row)
            lines.append(jnp.where((lane > base + p) & (lane < base + 8), 0.0, line))
        result = lines[7]
        for p in range(7):
            result = jnp.where(sub == p, lines[p], result)
        groups[own] = result
        inside = (lane >= base) & (lane < base + 8)
        for k in range(own + 1, size // 8):
            old = groups[k]
            new = jnp.where(inside, 0.0, old)
            parts = []
            for p in range(8):
                part = jnp.broadcast_to(old[:, base + p : base + p + 1], whole)
                for before in range(p):
                    part = part - parts[before] * factor[before][p]
                part = part * roots[p]
                parts.append(part)
                new = new - part * lines[p]
            groups[k] = new
    for k in range(size // 8):
        inverse[8 * k : 8 * k + 8, :] = jnp.where(lane <= sub + 8 * k, groups[k], 0.0) * scale
    start = pl.multiple_of(lax.axis_index("cols") * 64, 64)
    lower = inverse[pl.ds(start, 64), :]
    for i in range(4):
        at = slice(i * 512, i * 512 + 512)
        modes[:, at] = jnp.dot(
            lower,
            jnp.transpose(second[at, :]),
            precision=lax.Precision.HIGHEST,
            preferred_element_type=jnp.float32,
        )


def fast_body(sketch, geometry, neighbours, counts):
    rows_n = lax.axis_size("rows")
    wavenumber = 4.0 * math.sqrt(B)
    levels = 1 + rows_n.bit_length() - 1
    vmem = pl.BlockSpec(memory_space=pltpu.VMEM)
    hbm = pl.BlockSpec(memory_space=pltpu.HBM)
    gram, second = pl.pallas_call(
        functools.partial(fast_kernel, rows_n, wavenumber),
        name="sketch_twice",
        out_shape=(
            jax.ShapeDtypeStruct((128, 128), jnp.float32),
            jax.ShapeDtypeStruct((2 * B, 128), jnp.float32),
        ),
        in_specs=[hbm, hbm, hbm, hbm],
        out_specs=(vmem, vmem),
        scratch_shapes=[
            pltpu.VMEM((B, SLOTS * B), jnp.bfloat16),
            pltpu.VMEM((128, SLOTS * B), jnp.bfloat16),
            pltpu.VMEM((3, SLOTS * B), jnp.float32),
            pltpu.VMEM((3, SLOTS * B), jnp.float32),
            pltpu.VMEM((SLOTS * B, 128), jnp.bfloat16),
            pltpu.VMEM((B, 128), jnp.float32),
            pltpu.VMEM((B, 128), jnp.float32),
            pltpu.VMEM((B, 128), jnp.float32),
            pltpu.VMEM((128, 128), jnp.float32),
            pltpu.VMEM((levels, 64, 128), jnp.float32),
            pltpu.VMEM((levels, 64, 128), jnp.float32),
            pltpu.SemaphoreType.DMA((2, 2)),
            pltpu.SemaphoreType.DMA((2, 6)),
            pltpu.SemaphoreType.DMA((2, 4, B // CHUNK)),
            pltpu.SemaphoreType.DMA((2, levels + 1)),
            pltpu.SemaphoreType.DMA((2, B // CHUNK)),
            pltpu.SemaphoreType.DMA((4,)),
            pltpu.SMEM((SLOTS, 2 * rows_n), jnp.int32),
            pltpu.SMEM((2 * rows_n,), jnp.int32),
        ],
        compiler_params=pltpu.CompilerParams(
            collective_id=0, has_side_effects=True, vmem_limit_bytes=48 * 1024 * 1024
        ),
    )(sketch, geometry, jnp.transpose(neighbours), counts)
    scale = math.sqrt(2 * B * rows_n)
    return pl.pallas_call(
        functools.partial(finish_kernel, scale),
        name="orthonormal_rows",
        out_shape=jax.ShapeDtypeStruct((64, 2 * B), jnp.float32),
        in_specs=[vmem, vmem],
        out_specs=vmem,
        scratch_shapes=[pltpu.VMEM((128, 128), jnp.float32)],
        compiler_params=pltpu.CompilerParams(vmem_limit_bytes=16 * 1024 * 1024),
    )(gram, second)


def solution(mesh):
    rows_n, cols_n = mesh.shape["rows"], mesh.shape["cols"]
    pair = cols_n == 2 and rows_n > 1 and rows_n & (rows_n - 1) == 0
    return jax.shard_map(
        fast_body if pair else body,
        mesh=mesh,
        in_specs=(P("cols", "rows"), P(None, "rows"), P(), P()),
        out_specs=P("cols", "rows"),
        check_vma=False,
    )
```

```python
import functools
import math

import jax
import jax.numpy as jnp
from jax import lax
from jax.experimental import pallas as pl
from jax.experimental.pallas import tpu as pltpu
from jax.sharding import PartitionSpec as P

B = 1024
BLK_DEV = 2


highest = lax.Precision.HIGHEST


def padded(shard, sides, width):
    for axis, dim in sides:
        size, length = (lax.axis_size(axis), shard.shape[dim])
        up = [(i, (i + 1) % size) for i in range(size - 1)]
        down = [(j, i) for i, j in up]
        last = lax.slice_in_dim(shard, length - width, length, axis=dim)
        initial = lax.slice_in_dim(shard, 0, width, axis=dim)
        before = lax.ppermute(last, axis, up)
        after = lax.ppermute(initial, axis, down)
        shard = jnp.concatenate([before, shard, after], axis=dim)
    return shard


def spread(value, axis, source):
    kept = jnp.where(lax.axis_index(axis) == source, value, 0).astype(value.dtype)
    return lax.psum(kept, axis)


def kernel_tile(col_geo, row_geo, wavenumber):
    delta_x = col_geo[0][:, None] - row_geo[0][None, :]
    delta_y = col_geo[1][:, None] - row_geo[1][None, :]
    distance = jnp.sqrt(delta_x * delta_x + delta_y * delta_y)
    weights = col_geo[2][:, None] * row_geo[2][None, :]
    return (weights * jnp.sinc(distance * (wavenumber / math.pi))).astype(jnp.bfloat16)


def choose_slice(own_array, start, width):
    own_part = lax.dynamic_slice_in_dim(own_array, start, width, 1)
    return own_part


def task_lists(neighbours, counts, device_index, unit_blocks):
    slot_count = neighbours.shape[1]
    unit_count = unit_blocks.shape[0]
    slot_ids = jnp.arange(slot_count, dtype=jnp.int32)
    owners = jnp.zeros((unit_count,), jnp.int32) + device_index
    row_blocks = owners * BLK_DEV + unit_blocks
    flags = (slot_ids[None, :] < counts[row_blocks][:, None]).astype(jnp.int32).reshape(-1)
    column_ids = neighbours[row_blocks].reshape(-1)
    base_blocks = jnp.repeat(owners * BLK_DEV - BLK_DEV, slot_count)
    starts = (column_ids - base_blocks) * B
    task_total = flags.shape[0]
    task_ids = jnp.arange(task_total, dtype=jnp.int32)
    rank = jnp.cumsum(flags) - flags
    taken = flags == 1
    task_sides = jnp.zeros((task_total,), jnp.int32)
    target = jnp.where(taken, rank, task_total)
    blank = jnp.zeros((task_total + 1,), jnp.int32)
    order_side = blank.at[target].set(task_sides)
    order_unit = blank.at[target].set(task_ids // slot_count % unit_count)
    order_start = blank.at[target].set(starts)
    return (order_side, order_unit, order_start, jnp.sum(taken.astype(jnp.int32)))


def evaluate_tiles(tables, geo_wide, unit_blocks, unit_offset, unit_rows, capacity, wavenumber):
    order_side, order_unit, order_start, own_count = tables

    def add_tile(task, stored):
        row_start = (BLK_DEV + unit_blocks[order_unit[task]]) * B + unit_offset
        row_geo = choose_slice(geo_wide, row_start, unit_rows)
        col_geo = choose_slice(geo_wide, order_start[task], B)
        tile = kernel_tile(col_geo, row_geo, wavenumber)
        return lax.dynamic_update_slice(stored, tile[None], (task, 0, 0))

    initial = jnp.zeros((capacity, B, unit_rows), jnp.bfloat16)
    return lax.fori_loop(0, own_count, add_tile, initial)


def apply_tiles(stored, tables, panel_wide, unit_rows, unit_count):
    order_side, order_unit, order_start, own_count = tables
    columns = panel_wide.shape[0]
    side_count = 1

    def add_term(task, running):
        col_panel = choose_slice(panel_wide, order_start[task], B)
        term = jnp.dot(col_panel, stored[task], preferred_element_type=jnp.float32)
        return running + term[None]

    initial = jnp.zeros((side_count, columns, unit_count * unit_rows), jnp.float32)
    return lax.fori_loop(0, own_count, add_term, initial)


def operator_product(panel_t, stored, tables, unit_rows, unit_count):
    panel_wide = padded(panel_t, (("rows", 1),), BLK_DEV * B)
    gathered = apply_tiles(
        stored,
        tables,
        lax.all_gather(panel_wide, "cols", axis=0, tiled=True),
        unit_rows,
        unit_count,
    )[0]
    return lax.all_to_all(gathered, "cols", split_axis=0, concat_axis=1, tiled=True)


def normalize(current):
    gram_matrix = lax.psum(jnp.dot(current, current.T, precision=highest), "rows")
    cholesky_factor = jnp.linalg.cholesky(gram_matrix)
    return lax.linalg.triangular_solve(cholesky_factor, current, left_side=True, lower=True)


def orthonormal(second_product):
    position = lax.axis_index("cols")
    panels = lax.axis_size("cols")
    norm_scale = math.sqrt(second_product.shape[1] * lax.axis_size("rows"))
    mode_rows = jnp.zeros_like(second_product)
    removed = jnp.zeros_like(second_product)
    for panel_index in range(panels):
        basis_rows = normalize(second_product - removed)
        mode_rows = jnp.where(position == panel_index, basis_rows, mode_rows)
        if panel_index + 1 < panels:
            finished = spread(basis_rows, "cols", panel_index)
            coefficients = lax.psum(jnp.dot(finished, second_product.T, precision=highest), "rows")
            update = jnp.dot(coefficients.T, finished, precision=highest)
            removed = removed + jnp.where(position > panel_index, update, 0.0)
    return mode_rows * norm_scale


def body(sketch, geometry, neighbours, counts):
    wavenumber = 4.0 * math.sqrt(B)
    device_index = lax.axis_index("rows")
    geo_wide = padded(geometry, (("rows", 1),), BLK_DEV * B)
    unit_blocks = jnp.arange(BLK_DEV, dtype=jnp.int32)
    unit_offset = 0
    unit_rows = BLK_DEV * B // lax.axis_size("cols")
    slice_start = lax.axis_index("cols") * unit_rows
    unit_blocks = jnp.reshape(slice_start // B, (1,))
    unit_offset = slice_start % B
    unit_count = unit_blocks.shape[0]
    tables = task_lists(neighbours, counts, device_index, unit_blocks)
    capacity = unit_count * neighbours.shape[1]
    stored = evaluate_tiles(
        tables, geo_wide, unit_blocks, unit_offset, unit_rows, capacity, wavenumber
    )
    first_product = operator_product(sketch, stored, tables, unit_rows, unit_count).astype(
        jnp.bfloat16
    )
    second_product = operator_product(first_product, stored, tables, unit_rows, unit_count)
    return orthonormal(second_product)


MESH = pl.DeviceIdType.MESH
SLOTS = 5
CHUNK = 256
GROUP = 256
SIN = (
    6.2830557981504445,
    -41.331214276596405,
    81.36681478361689,
    -74.47800141803688,
    32.781394500276015,
)
MAGIC = 12582912.0


def column_range(dq, to_col):
    first = -2 * dq - to_col + 2
    kept = [e for e in range(2) if 0 <= first + e < SLOTS]
    lo, count = kept[0], len(kept)
    return (first + lo) * B, lo * B, count * B


def fast_kernel(
    rows_n,
    wavenumber,
    sketch,
    geometry,
    neighbours_hbm,
    counts_hbm,
    gram,
    second,
    tiles,
    wide,
    geo,
    weight,
    first,
    own_x,
    own_y,
    own_a,
    gram_sum,
    gram_send,
    gram_recv,
    geo_sem,
    sk_sem,
    first_sem,
    gram_sem,
    pair_sem,
    local_sem,
    neighbours,
    counts,
):
    q = lax.axis_index("rows")
    x = lax.axis_index("cols")
    r = 2 * q + x
    blocks_n = 2 * rows_n
    flips = [1 << k for k in range(rows_n.bit_length() - 1)]

    def partner_q(flip):
        return q + flip - 2 * flip * ((q // flip) % 2)

    barrier = pltpu.get_barrier_semaphore()
    pl.semaphore_signal(barrier, inc=1, device_id=(q, 1 - x), device_id_type=MESH)
    for flip in flips[1:]:
        pl.semaphore_signal(barrier, inc=1, device_id=(partner_q(flip), x), device_id_type=MESH)
    for dq in (-1, 1):

        @pl.when((q + dq >= 0) & (q + dq < rows_n))
        def _(dq=dq):
            pl.semaphore_signal(barrier, inc=1, device_id=(q + dq, x), device_id_type=MESH)

    def local_copy(c, k):
        at = column_range(0, c)[0]
        if k == 0:
            return pltpu.make_async_copy(geometry, geo.at[:, at : at + 2 * B], local_sem.at[0])
        held = wide.at[64 * c : 64 * c + 64, at : at + 2 * B]
        return pltpu.make_async_copy(sketch, held, local_sem.at[1])

    table_copies = (
        pltpu.make_async_copy(neighbours_hbm, neighbours, local_sem.at[2]),
        pltpu.make_async_copy(counts_hbm, counts, local_sem.at[3]),
    )
    for copy in table_copies:
        copy.start()
    for c in range(2):

        @pl.when(x == c)
        def _(c=c):
            local_copy(c, 0).start()
            local_copy(c, 1).start()

    for step in (-2, -1, 1, 2):

        @pl.when((r + step < 0) | (r + step >= blocks_n))
        def _(step=step):
            at = (2 + step) * B
            geo[:, at : at + B] = jnp.full((3, B), -1.0, jnp.float32)
            wide[:, at : at + B] = jnp.zeros((128, B), jnp.bfloat16)
            first[at : at + B, :] = jnp.zeros((B, 128), jnp.bfloat16)

    sides = jnp.where(q > 0, 1, 0) + jnp.where(q < rows_n - 1, 1, 0)
    pl.semaphore_wait(barrier, len(flips) + sides)

    def geo_copy(dq, col):
        to, lo, n = column_range(dq, col)
        k = (dq + 1) // 2
        return pltpu.make_async_remote_copy(
            src_ref=geometry.at[:, lo : lo + n],
            dst_ref=geo.at[:, to : to + n],
            send_sem=geo_sem.at[0, k],
            recv_sem=geo_sem.at[1, k],
            device_id=(q + dq, x),
            device_id_type=MESH,
        )

    def cross_copy(c):
        at = column_range(0, 1 - c)[0]
        return pltpu.make_async_remote_copy(
            src_ref=sketch,
            dst_ref=wide.at[64 * c : 64 * c + 64, at : at + 2 * B],
            send_sem=sk_sem.at[0, 0],
            recv_sem=sk_sem.at[1, 0],
            device_id=(q, 1 - c),
            device_id_type=MESH,
        )

    def side_copy(dq, c, passed_on):
        to, lo, n = column_range(dq, c)
        k = (1 if dq < 0 else 2) + (2 if passed_on else 0)
        panel = 1 - c if passed_on else c
        lines = slice(64 * panel, 64 * panel + 64)
        at = column_range(0, c)[0] + lo
        return pltpu.make_async_remote_copy(
            src_ref=wide.at[lines, at : at + n] if passed_on else sketch.at[:, lo : lo + n],
            dst_ref=wide.at[lines, to : to + n],
            send_sem=sk_sem.at[0, k],
            recv_sem=sk_sem.at[1, k],
            device_id=(q + dq, c),
            device_id_type=MESH,
        )

    def inside(dq):
        return (q + dq >= 0) & (q + dq < rows_n)

    for c in range(2):
        for dq in (-1, 1):

            @pl.when((x == c) & inside(dq))
            def _(c=c, dq=dq):
                geo_copy(dq, c).start()

    for c in range(2):

        @pl.when(x == c)
        def _(c=c):
            cross_copy(c).start()

        for dq in (-1, 1):

            @pl.when((x == c) & inside(dq))
            def _(c=c, dq=dq):
                side_copy(dq, c, False).start()

    def pass_sketch_on():
        for c in range(2):

            @pl.when(x == c)
            def _(c=c):
                cross_copy(1 - c).wait_recv()

            for dq in (-1, 1):

                @pl.when((x == c) & inside(dq))
                def _(c=c, dq=dq):
                    side_copy(dq, c, True).start()

    for c in range(2):

        @pl.when(x == c)
        def _(c=c):
            local_copy(c, 0).wait()

    to_turns = wavenumber / (2.0 * math.pi)

    def scale_window(at):
        base = (r - 2).astype(jnp.float32)
        weight[0:1, at] = (geo[0:1, at] - base) * to_turns
        weight[1:2, at] = geo[1:2, at] * to_turns

    scale_window(slice(2 * B, 3 * B))
    weight[2:3, 2 * B : 3 * B] = geo[2:3, 2 * B : 3 * B]

    def spread_own(i, carry):
        cols = pl.ds(pl.multiple_of(2 * B + i * 128, 128), 128)
        at = pl.ds(pl.multiple_of(i * 128, 128), 128)
        for row, ref in ((0, own_x), (1, own_y), (2, own_a)):
            line = jnp.broadcast_to(weight[row : row + 1, cols], (128, 128))
            ref[at, :] = jnp.transpose(line)
        return carry

    lax.fori_loop(0, B // 128, spread_own, 0)

    def wait_geo():
        for c in range(2):
            for dq in (-1, 1):

                @pl.when((x == c) & inside(-dq))
                def _(c=c, dq=dq):
                    geo_copy(dq, c).wait_recv()

    def mask_weights():
        for slot in range(SLOTS):
            hit = jnp.float32(0.0)
            for s in range(SLOTS):
                found = (neighbours[s, r] == r + slot - 2) & (s < counts[r])
                hit = jnp.maximum(hit, jnp.where(found, jnp.float32(1.0), jnp.float32(0.0)))
            at = slice(slot * B, slot * B + B)
            scale_window(at)
            weight[2:3, at] = geo[2:3, at] * (hit * (0.5 / math.pi))

    tiny = 2.5e-10

    def evaluate(i):
        def one(g, carry, width=GROUP):
            cols = pl.ds(pl.multiple_of(g * width, width), width)
            col_x, col_y, col_a = weight[0:1, cols], weight[1:2, cols], weight[2:3, cols]
            for h in range(CHUNK // 128):
                at = pl.ds(pl.multiple_of(i * CHUNK + h * 128, 128), 128)
                for lane in range(width // 128):
                    part = slice(lane * 128, lane * 128 + 128)
                    dx = own_x[at, :] - col_x[:, part]
                    dy = own_y[at, :] - col_y[:, part]
                    square = jnp.maximum(dx * dx + dy * dy, tiny)
                    inv = lax.rsqrt(square)
                    turns = square * inv
                    f = turns - ((turns + MAGIC) - MAGIC)
                    z = f * f
                    poly = jnp.float32(SIN[4])
                    for coefficient in SIN[3::-1]:
                        poly = poly * z + coefficient
                    value = (poly * f) * inv * (own_a[at, :] * col_a[:, part])
                    lanes = pl.ds(pl.multiple_of(g * width + lane * 128, 128), 128)
                    tiles[at, lanes] = value.astype(jnp.bfloat16)
            return carry

        per_block = B // GROUP

        def outside(g, carry):
            return one(jnp.where(g < 2, g, g + 1), carry, B)

        lax.fori_loop(0, 4, outside, 0)
        lax.fori_loop(2 * per_block + i, 3 * per_block, one, 0)

        def mirror(g, carry):
            at = pl.ds(pl.multiple_of(i * CHUNK, CHUNK), CHUNK)
            rows = pl.ds(pl.multiple_of(g * CHUNK, CHUNK), CHUNK)
            to = pl.ds(pl.multiple_of(2 * B + g * CHUNK, CHUNK), CHUNK)
            cols = pl.ds(pl.multiple_of(2 * B + i * CHUNK, CHUNK), CHUNK)
            tiles[at, to] = jnp.transpose(tiles[rows, cols])
            return carry

        lax.fori_loop(0, i, mirror, 0)

    onward = 1 - 2 * x

    def first_copy(i, k):
        held = (2, 2, 2, 3 - 2 * x)[k]
        slot = (4, 0, 1 + 2 * x, 1 + 2 * x)[k]
        target = ((q - 1, x), (q + 1, x), (q, 1 - x), (q + onward, x))[k]
        rows = pl.ds(pl.multiple_of(held * B + i * CHUNK, CHUNK), CHUNK)
        to = pl.ds(pl.multiple_of(slot * B + i * CHUNK, CHUNK), CHUNK)
        return pltpu.make_async_remote_copy(
            src_ref=first.at[rows, :],
            dst_ref=first.at[to, :],
            send_sem=first_sem.at[0, k, i],
            recv_sem=first_sem.at[1, k, i],
            device_id=target,
            device_id_type=MESH,
        )

    def sends(k):
        return (q > 0, q < rows_n - 1, None, inside(onward))[k]

    def receives(k):
        return (q < rows_n - 1, q > 0, None, inside(-onward))[k]

    def guarded(condition, action):
        if condition is None:
            action()
        else:
            pl.when(condition)(action)

    def pass_first_on(i):
        first_copy(i, 2).wait_recv()
        guarded(sends(3), lambda: first_copy(i, 3).start())

    def product_and_send(i):
        at = pl.ds(pl.multiple_of(i * CHUNK, CHUNK), CHUNK)
        part = lax.dot_general(
            tiles[at, :],
            wide[...],
            (((1,), (1,)), ((), ())),
            preferred_element_type=jnp.float32,
        )
        rows = pl.ds(pl.multiple_of(2 * B + i * CHUNK, CHUNK), CHUNK)
        first[rows, :] = part.astype(jnp.bfloat16)
        for k in (2, 0, 1):
            guarded(sends(k), lambda k=k: first_copy(i, k).start())

    wait_geo()
    for copy in table_copies:
        copy.wait()
    mask_weights()
    chunks = B // CHUNK
    early = chunks - 1

    def eval_only(i, carry):
        evaluate(i)
        return carry

    lax.fori_loop(0, 1, eval_only, 0)
    pass_sketch_on()
    lax.fori_loop(1, early, eval_only, 0)

    for c in range(2):

        @pl.when(x == c)
        def _(c=c):
            local_copy(c, 1).wait()

        for dq in (-1, 1):

            @pl.when((x == c) & inside(-dq))
            def _(c=c, dq=dq):
                side_copy(dq, c, False).wait_recv()
                side_copy(dq, c, True).wait_recv()

    def product_only(i, carry):
        product_and_send(i)
        return carry

    lax.fori_loop(0, early, product_only, 0)

    def both(i, carry):
        evaluate(i)
        product_and_send(i)
        return carry

    lax.fori_loop(early, chunks, both, 0)

    def pass_chunk(i, carry):
        pass_first_on(i)
        return carry

    lax.fori_loop(0, chunks, pass_chunk, 0)

    def first_wait(i, carry):
        for k in range(4):
            if k != 2:
                guarded(receives(k), lambda k=k: first_copy(i, k).wait_recv())
            guarded(sends(k), lambda k=k: first_copy(i, k).wait_send())
        return carry

    lax.fori_loop(0, chunks, first_wait, 0)

    def pair_copy(i):
        rows = pl.ds(pl.multiple_of(x * B + i * CHUNK, CHUNK), CHUNK)
        return pltpu.make_async_remote_copy(
            src_ref=second.at[rows, :],
            dst_ref=second.at[rows, :],
            send_sem=pair_sem.at[0, i],
            recv_sem=pair_sem.at[1, i],
            device_id=(q, 1 - x),
            device_id_type=MESH,
        )

    def second_product(i, carry):
        at = pl.ds(pl.multiple_of(i * CHUNK, CHUNK), CHUNK)
        to = pl.ds(pl.multiple_of(x * B + i * CHUNK, CHUNK), CHUNK)
        part = jnp.dot(tiles[at, :], first[...], preferred_element_type=jnp.float32)
        second[to, :] = part
        pair_copy(i).start()
        turned = jnp.transpose(part)
        product = jnp.dot(
            turned, part, precision=lax.Precision.HIGHEST, preferred_element_type=jnp.float32
        )
        gram_sum[...] += product
        return carry

    gram_sum[...] = jnp.zeros((128, 128), jnp.float32)
    lax.fori_loop(0, chunks, second_product, 0)

    def exchange(src, dst, k, target):
        copy = pltpu.make_async_remote_copy(
            src_ref=src,
            dst_ref=dst,
            send_sem=gram_sem.at[0, k],
            recv_sem=gram_sem.at[1, k],
            device_id=target,
            device_id_type=MESH,
        )
        copy.start()
        copy.wait()

    mine = pl.ds(pl.multiple_of((q % 2) * 64, 64), 64)
    theirs = pl.ds(pl.multiple_of((1 - q % 2) * 64, 64), 64)
    exchange(gram_sum.at[theirs, :], gram_recv.at[0], 0, (partner_q(1), x))
    gram_send[0] = gram_sum[mine, :] + gram_recv[0]
    targets = [(partner_q(flip), x) for flip in flips[1:]] + [(q, 1 - x)]
    for k, target in enumerate(targets):
        exchange(gram_send.at[k], gram_recv.at[k + 1], k + 1, target)
        gram_send[k + 1] = gram_send[k] + gram_recv[k + 1]
    last = len(targets)
    gram[mine, :] = gram_send[last]
    exchange(gram_send.at[last], gram.at[mine, :], last + 1, (partner_q(1), x))

    for c in range(2):
        for dq in (-1, 1):

            @pl.when((x == c) & inside(dq))
            def _(c=c, dq=dq):
                geo_copy(dq, c).wait_send()

    for c in range(2):

        @pl.when(x == c)
        def _(c=c):
            cross_copy(c).wait_send()

        for dq in (-1, 1):

            @pl.when((x == c) & inside(dq))
            def _(c=c, dq=dq):
                side_copy(dq, c, False).wait_send()
                side_copy(dq, c, True).wait_send()

    def pair_wait(i, carry):
        pair_copy(i).wait()
        return carry

    lax.fori_loop(0, chunks, pair_wait, 0)


def finish_kernel(scale, gram, second, modes, inverse):
    size = gram.shape[0]
    lane = lax.broadcasted_iota(jnp.int32, (8, size), 1)
    sub = lax.broadcasted_iota(jnp.int32, (8, size), 0)
    groups = [gram[8 * k : 8 * k + 8, :] for k in range(size // 8)]
    whole = (8, size)
    for own in range(size // 8):
        base = 8 * own
        block = groups[own]
        column = [jnp.broadcast_to(block[:, base + c : base + c + 1], whole) for c in range(8)]
        roots, factor, lines = [], [], []
        for p in range(8):
            root = lax.rsqrt(jnp.broadcast_to(column[p][p : p + 1, :], whole))
            scaled = column[p] * root
            row = {}
            for c in range(p + 1, 8):
                row[c] = jnp.broadcast_to(column[c][p : p + 1, :], whole) * root
                column[c] = column[c] - scaled * row[c]
            line = jnp.broadcast_to(block[p : p + 1, :], whole)
            line = jnp.where(lane == base + p, 1.0, line) * root
            new = jnp.where(lane == base + p, 0.0, block) - scaled * line
            block = jnp.where(sub > p, new, block)
            roots.append(root)
            factor.append(row)
            lines.append(jnp.where((lane > base + p) & (lane < base + 8), 0.0, line))
        result = lines[7]
        for p in range(7):
            result = jnp.where(sub == p, lines[p], result)
        groups[own] = result
        inside = (lane >= base) & (lane < base + 8)
        for k in range(own + 1, size // 8):
            old = groups[k]
            new = jnp.where(inside, 0.0, old)
            parts = []
            for p in range(8):
                part = jnp.broadcast_to(old[:, base + p : base + p + 1], whole)
                for before in range(p):
                    part = part - parts[before] * factor[before][p]
                part = part * roots[p]
                parts.append(part)
                new = new - part * lines[p]
            groups[k] = new
    for k in range(size // 8):
        inverse[8 * k : 8 * k + 8, :] = jnp.where(lane <= sub + 8 * k, groups[k], 0.0) * scale
    start = pl.multiple_of(lax.axis_index("cols") * 64, 64)
    lower = inverse[pl.ds(start, 64), :]
    for i in range(4):
        at = slice(i * 512, i * 512 + 512)
        modes[:, at] = jnp.dot(
            lower,
            jnp.transpose(second[at, :]),
            precision=lax.Precision.HIGHEST,
            preferred_element_type=jnp.float32,
        )


def fast_body(sketch, geometry, neighbours, counts):
    rows_n = lax.axis_size("rows")
    wavenumber = 4.0 * math.sqrt(B)
    levels = 1 + rows_n.bit_length() - 1
    vmem = pl.BlockSpec(memory_space=pltpu.VMEM)
    hbm = pl.BlockSpec(memory_space=pltpu.HBM)
    gram, second = pl.pallas_call(
        functools.partial(fast_kernel, rows_n, wavenumber),
        name="sketch_twice",
        out_shape=(
            jax.ShapeDtypeStruct((128, 128), jnp.float32),
            jax.ShapeDtypeStruct((2 * B, 128), jnp.float32),
        ),
        in_specs=[hbm, hbm, hbm, hbm],
        out_specs=(vmem, vmem),
        scratch_shapes=[
            pltpu.VMEM((B, SLOTS * B), jnp.bfloat16),
            pltpu.VMEM((128, SLOTS * B), jnp.bfloat16),
            pltpu.VMEM((3, SLOTS * B), jnp.float32),
            pltpu.VMEM((3, SLOTS * B), jnp.float32),
            pltpu.VMEM((SLOTS * B, 128), jnp.bfloat16),
            pltpu.VMEM((B, 128), jnp.float32),
            pltpu.VMEM((B, 128), jnp.float32),
            pltpu.VMEM((B, 128), jnp.float32),
            pltpu.VMEM((128, 128), jnp.float32),
            pltpu.VMEM((levels, 64, 128), jnp.float32),
            pltpu.VMEM((levels, 64, 128), jnp.float32),
            pltpu.SemaphoreType.DMA((2, 2)),
            pltpu.SemaphoreType.DMA((2, 6)),
            pltpu.SemaphoreType.DMA((2, 4, B // CHUNK)),
            pltpu.SemaphoreType.DMA((2, levels + 1)),
            pltpu.SemaphoreType.DMA((2, B // CHUNK)),
            pltpu.SemaphoreType.DMA((4,)),
            pltpu.SMEM((SLOTS, 2 * rows_n), jnp.int32),
            pltpu.SMEM((2 * rows_n,), jnp.int32),
        ],
        compiler_params=pltpu.CompilerParams(
            collective_id=0, has_side_effects=True, vmem_limit_bytes=48 * 1024 * 1024
        ),
    )(sketch, geometry, jnp.transpose(neighbours), counts)
    scale = math.sqrt(2 * B * rows_n)
    return pl.pallas_call(
        functools.partial(finish_kernel, scale),
        name="orthonormal_rows",
        out_shape=jax.ShapeDtypeStruct((64, 2 * B), jnp.float32),
        in_specs=[vmem, vmem],
        out_specs=vmem,
        scratch_shapes=[pltpu.VMEM((128, 128), jnp.float32)],
        compiler_params=pltpu.CompilerParams(vmem_limit_bytes=16 * 1024 * 1024),
    )(gram, second)


def solution(mesh):
    rows_n, cols_n = mesh.shape["rows"], mesh.shape["cols"]
    pair = cols_n == 2 and rows_n > 1 and rows_n & (rows_n - 1) == 0
    return jax.shard_map(
        fast_body if pair else body,
        mesh=mesh,
        in_specs=(P("cols", "rows"), P(None, "rows"), P(), P()),
        out_specs=P("cols", "rows"),
        check_vma=False,
    )
```
